32 devices in a mesh: groups: 2 (over x), win: 4 (over z), lat: 4 (over y, core).
Axes of the slice: x: 2, y: 2, z: 4, core: 2. Of those that a mesh axis runs over, the one named last changes fastest.
Arguments:
- thickness: float32 [8, 2, 3, 8, 64, 256], P(('groups', 'win'), None, None, None, 'lat'), parts along dimension 0, may hold values from 0.5 to 1.5
- obs_cells: int32 [8, 2, 1024], P(('groups', 'win'), None, 'lat'), parts along dimension 0, may hold values from 0 to 4095
- obs_values: float32 [8, 2, 1024], P(('groups', 'win'), None, 'lat'), parts along dimension 0, may hold values from -6 to 6
- ocean_mask: int32 [128, 256], P(('groups', 'lat')), parts along dimension 0, may hold values 0 or 1
- coupling: float32 [8, 8], replicated, may hold values from -1.2 to 1.2
- damping: float32 [8], replicated, may hold values from 0.05 to 0.8
Outputs:
- window_adjoint: float32 [8, 3, 8, 64, 256], P(('groups', 'win'), None, None, 'lat'), parts along dimension 0
- bias_gradient: float32 [16, 64, 256], P('groups', 'lat'), parts along dimension 0
The draws below stay inside these ranges and needn't reach their ends.
There are 2 independent parts, one for each index of `groups`. The reference program is written for one: setup_inputs(seed, part) draws one part's arguments, and reference() takes and returns one part's arrays. A program takes and returns all parts, laid end to end along the dimension named above; an argument that names none is the same for every part. Nothing has to cross between parts.
Inputs may be any that keep to these rules, and one draw needn't show every extreme that they name: `obs_cells`: entry k of a step's list names a cell of the latitude block that starts at row (k // 256) * 16, as row * 256 + column within that block; a cell may be named several times.
All inputs are finite; a program needn't handle non-finite values. No bound on the sum of `ocean_mask` on one device may be relied on, other than what follows from the above.
Results may differ from the reference program's by a relative error of at most 0.00011.
Values sent between devices are 32-bit elements; how exact they have to be, the bound alone decides.
No kernel may reach another device: no remote copies, remote signals or barrier semaphores. Data moves between devices by JAX's collectives and lax.ppermute only.
A program may use at most 64 MiB of HBM per device.

```python
import math
import jax
import jax.numpy as jnp
from jax import lax

LAYERS = 8
ROWS_DEV = 16
COLS = 256
STEPS = 2
OBS_DEV = 256
NSUB = 4
ROWS = 64
OBS = 1024


def with_ends(values, rng, low, largest):
    extent = values.shape
    place = [jax.random.randint(jax.random.fold_in(rng, axis), (), 0, extent[axis]) for axis in range(len(extent))]
    values = values.at[tuple(place)].set(low)
    longest = extent.index(max(extent))
    place[longest] = (place[longest] + 1) % extent[longest]
    return values.at[tuple(place)].set(largest)


def block_levels(key, dims, cuts, low, high):
    def one(dim, parts):
        draws = jax.random.uniform(jax.random.fold_in(jax.random.fold_in(key, 6), dim), (parts,), jnp.float32, low / len(cuts), high / len(cuts))
        return jnp.repeat(jnp.exp(draws), dims[dim] // parts).reshape((-1,) + (1,) * (len(dims) - dim - 1))

    factor_of = one(*cuts[0])
    for cut in cuts[1:]:
        factor_of = factor_of * one(*cut)
    return factor_of


def noise(own_key, dims, spread, limit, shards=(), kind=jnp.bfloat16):
    drawn = spread * jax.random.normal(own_key, dims, jnp.float32)
    if shards:
        drawn = drawn * block_levels(own_key, dims, shards, -0.22, 0.18)
    return jnp.clip(drawn, -limit, limit).astype(kind)


def setup_inputs(seed: int = 0, part: int = 0) -> dict:
    seeds = jax.random.split(jax.random.key(seed), 7)
    part_keys = jax.random.split(jax.random.fold_in(seeds[6], part), 7)
    thickness = jnp.clip(0.5 + 1.0 * jax.random.uniform(part_keys[0], (NSUB, STEPS, 3, LAYERS, ROWS, COLS), jnp.float32) ** block_levels(part_keys[0], (NSUB, STEPS, 3, LAYERS, ROWS, COLS), ((0, 4), (4, 4)), -0.2, 0.2), 0.5, 1.5)
    obs_cells = with_ends(jax.random.randint(part_keys[1], (NSUB, STEPS, OBS), 0, ROWS_DEV * COLS), jax.random.fold_in(part_keys[1], 1), 0, (ROWS_DEV * COLS) - 1).astype(jnp.int32)
    obs_values = noise(part_keys[2], (NSUB, STEPS, OBS), 1.0, 6.0, ((0, 4), (2, 4)), jnp.float32)
    ocean_mask = with_ends((jax.random.randint(part_keys[3], (ROWS, COLS), 0, 8) < 7).astype(jnp.int32), jax.random.fold_in(part_keys[3], 1), 0, 1)
    coupling = noise(seeds[4], (LAYERS, LAYERS), 0.3, 1.2, (), jnp.float32)
    damping = jnp.clip(jnp.exp(jax.random.uniform(seeds[5], (LAYERS,), jnp.float32, math.log(0.05), math.log(0.8))), 0.05, 0.8)
    return {"thickness": thickness, "obs_cells": obs_cells, "obs_values": obs_values, "ocean_mask": ocean_mask, "coupling": coupling, "damping": damping}


STEP_DT = 0.2
THIRD = 1.0 / 3.0
TWO_THIRDS = 2.0 / 3.0


def tendency(state, ocean, fcor, edges, mix, rate):
    p_part = state[1]
    q_part = state[2]
    a_part = state[0]
    w_mid = edges[0][:, 1:-1]
    dxp = 0.5 * (jnp.roll(p_part, -1, axis=2) - jnp.roll(p_part, 1, axis=2))
    dyq = 0.5 * (edges[1][:, 2:] - edges[1][:, :-2])
    mixed = jnp.einsum("kl,krc->lrc", mix, dxp + dyq, precision=lax.Precision.HIGHEST)
    t_a = ocean * (mixed - rate * a_part)
    t_p = ocean * (0.5 * (jnp.roll(w_mid, -1, axis=2) - jnp.roll(w_mid, 1, axis=2)) + fcor * q_part - rate * p_part)
    t_q = ocean * (0.5 * (edges[0][:, 2:] - edges[0][:, :-2]) - fcor * p_part - rate * q_part)
    return jnp.stack([t_a, t_p, t_q])


def runge_kutta(state, section_tend):
    first = state + STEP_DT * section_tend(state, 0)
    second = 0.75 * state + 0.25 * (first + STEP_DT * section_tend(first, 1))
    return THIRD * state + TWO_THIRDS * (second + STEP_DT * section_tend(second, 2))


def add_obs(state, cells, values):
    layer_a = state[0]
    flat = layer_a.reshape(layer_a.shape[0], -1).at[:, cells].add(values[None, :])
    return state.at[0].set(flat.reshape(layer_a.shape))


def reference(thickness, obs_cells, obs_values, ocean_mask, coupling, damping):
    rows = ocean_mask.shape[0]
    ocean = ocean_mask.astype(jnp.float32)
    fcor = (0.3 + 0.4 * (jnp.arange(rows, dtype=jnp.float32) / rows - 0.5))[:, None]
    mix = jnp.eye(coupling.shape[0], dtype=jnp.float32) + coupling
    rate = damping[:, None, None]
    count = obs_cells.shape[2]
    offset = ((jnp.arange(count, dtype=jnp.int32) // OBS_DEV) * (ROWS_DEV * COLS)).astype(jnp.int32)
    lam = jnp.zeros((3,) + thickness.shape[3:], jnp.float32)
    bias = jnp.zeros(thickness.shape[3:], jnp.float32)
    starts = []
    for window in reversed(range(NSUB)):
        for step in reversed(range(STEPS)):
            lam = add_obs(lam, obs_cells[window, step] + offset, obs_values[window, step])
            thick = thickness[window, step]

            def section_tend(state, section):
                edges = jnp.stack([thick[section] * state[0], state[2]])
                edges = jnp.pad(edges, ((0, 0), (0, 0), (1, 1), (0, 0)))
                return tendency(state, ocean, fcor, edges, mix, rate)

            lam = runge_kutta(lam, section_tend)
            bias = bias + STEP_DT * lam[0]
        starts.append(lam)
    return jnp.stack(starts[::-1]), bias
```

```python
import functools

import jax
import jax.numpy as jnp
from jax import lax
from jax.experimental import pallas as pl
from jax.experimental.pallas import tpu as pltpu
from jax.sharding import PartitionSpec as P

STEP_DT = 0.2
THIRD = 1.0 / 3.0
TWO_THIRDS = 2.0 / 3.0
STAGES = 3
UNROLL = 8
SUBLANES = 8

VMEM = pl.BlockSpec(memory_space=pltpu.VMEM)
SMEM = pl.BlockSpec(memory_space=pltpu.SMEM)


class Sizes:
    def __init__(self, steps, layers, rows, cols):
        self.steps, self.layers, self.rows, self.cols = steps, layers, rows, cols
        self.halo = STAGES * steps
        self.ext = rows + 2 * self.halo
        self.first = [sum(self.halo - m for m in range(j)) for j in range(self.halo)]
        self.halo_rows = sum(self.halo - m for m in range(self.halo))
        self.tail = -(-(steps + 1) * self.halo // SUBLANES)
        self.packed = self.halo_rows + self.tail

    def section(self, j):
        step, stage = self.steps - 1 - j // STAGES, j % STAGES
        return (step * STAGES + stage) * self.layers * self.rows


def rows_first(z, ref, base):
    lines = []
    for tile in range(z.rows // SUBLANES):
        block = jnp.stack(
            [ref[base + l * z.rows + tile * SUBLANES : base + l * z.rows + (tile + 1) * SUBLANES, :] for l in range(z.layers)]
        )
        block = jnp.swapaxes(block, 0, 1)
        lines.extend(block[m] for m in range(SUBLANES))
    return lines


def layers_first(z, ref, start, lines):
    for tile in range(z.rows // SUBLANES):
        block = jnp.swapaxes(jnp.stack(lines[tile * SUBLANES : (tile + 1) * SUBLANES]), 0, 1)
        for l in range(z.layers):
            low = start + l * z.rows + tile * SUBLANES
            ref[low : low + SUBLANES, :] = block[l]


def pack_kernel(z, th_ref, cells_ref, values_ref, mask_ref, up_ref, down_ref, own_ref):
    count = cells_ref.shape[1]
    row_ids = lax.broadcasted_iota(jnp.int32, (z.rows, count), 0)
    col_ids = lax.broadcasted_iota(jnp.int32, (z.cols, count), 0)
    for order in range(z.steps):
        step = z.steps - 1 - order
        cells = cells_ref[step : step + 1, :]
        values = values_ref[step : step + 1, :]
        by_row = jnp.where(row_ids == cells // z.cols, values, 0.0)
        by_col = jnp.where(col_ids == cells % z.cols, 1.0, 0.0).astype(jnp.bfloat16)
        field = jnp.zeros((z.rows, z.cols), jnp.float32)
        for _ in range(3):
            part = by_row.astype(jnp.bfloat16)
            by_row = by_row - part.astype(jnp.float32)
            field = field + lax.dot_general(
                part, by_col, (((1,), (1,)), ((), ())), preferred_element_type=jnp.float32
            )
        own_ref[order * z.rows : (order + 1) * z.rows, :] = field
    own_ref[z.steps * z.rows :, :] = mask_ref[...].astype(jnp.float32) * (0.5 * STEP_DT)
    for j in range(z.halo):
        lines, need = rows_first(z, th_ref, z.section(j)), z.halo - j
        for m in range(need):
            up_ref[z.first[j] + m] = lines[m]
            down_ref[z.first[j] + m] = lines[z.rows - need + m]
    for k in range(z.steps + 1):
        for m in range(z.halo):
            tile, line = divmod(k * z.halo + m, SUBLANES)
            start = k * z.rows
            up_ref[z.halo_rows + tile, line : line + 1, :] = own_ref[start + m : start + m + 1, :]
            last = start + z.rows - z.halo + m
            down_ref[z.halo_rows + tile, line : line + 1, :] = own_ref[last : last + 1, :]
    for q in range((z.steps + 1) * z.halo, z.tail * SUBLANES):
        tile, line = divmod(q, SUBLANES)
        for ref in (up_ref, down_ref):
            ref[z.halo_rows + tile, line : line + 1, :] = jnp.zeros((1, z.cols), jnp.float32)


def extend_kernel(z, coupling_ref, damping_ref, th_ref, above_ref, below_ref, own_ref, h_ref, obs_ref, oc_ref, keep_ref, mix_ref):
    layer_ids = lax.broadcasted_iota(jnp.int32, (z.layers, z.cols), 0)
    for j in range(z.layers):
        line = jnp.zeros((z.layers, z.cols), jnp.float32)
        for l in range(z.layers):
            k = (l - j) % z.layers
            weight = coupling_ref[k, l] + (1.0 if k == l else 0.0)
            line = jnp.where(layer_ids == l, weight, line)
        mix_ref[j * z.layers : (j + 1) * z.layers, :] = line
    rate = jnp.zeros((z.layers, z.cols), jnp.float32)
    for l in range(z.layers):
        rate = jnp.where(layer_ids == l, 2.0 * damping_ref[l], rate)

    shape = (z.layers, z.cols)

    def line_of(k, e):
        if e < z.halo:
            tile, line = divmod(k * z.halo + e, SUBLANES)
            return above_ref[z.halo_rows + tile, line : line + 1, :]
        if e >= z.halo + z.rows:
            tile, line = divmod(k * z.halo + e - z.halo - z.rows, SUBLANES)
            return below_ref[z.halo_rows + tile, line : line + 1, :]
        return own_ref[k * z.rows + e - z.halo : k * z.rows + e - z.halo + 1, :]

    for e in range(z.ext):
        for k in range(z.steps):
            obs_ref[k * z.ext + e] = jnp.broadcast_to(line_of(k, e), shape)
        oc = jnp.broadcast_to(line_of(z.steps, e), shape)
        oc_ref[e] = oc
        keep_ref[e] = 1.0 - oc * rate
    for j in range(z.halo):
        need = z.halo - j
        for m in range(need):
            h_ref[j * z.ext + j + m] = above_ref[z.first[j] + m]
            h_ref[j * z.ext + z.halo + z.rows + m] = below_ref[z.first[j] + m]
        for r, line in enumerate(rows_first(z, th_ref, z.section(j))):
            h_ref[j * z.ext + z.halo + r] = line


def over_rows(low, high, carry, body):
    turns = (high - low) // UNROLL

    def turn(t, carry):
        for u in range(UNROLL):
            carry = body(low + t * UNROLL + u, carry)
        return carry

    if turns > 1:
        carry = lax.fori_loop(0, turns, turn, carry)
        low = low + turns * UNROLL
    for row in range(low, high):
        carry = body(row, carry)
    return carry


def window_kernel(z, total_rows, first, *refs):
    if first:
        h_ref, obs_ref, oc_ref, keep_ref, mix_ref = refs[:5]
        refs = refs[5:]
    else:
        h_ref, obs_ref, oc_ref, keep_ref, mix_ref, main_in, above_in, below_in = refs[:8]
        refs = refs[8:]
    bias_ref, main_ref, top_ref, bottom_ref, x_ref, y_ref, w_ref, sum_ref = refs
    halo, ext, rows, layers = z.halo, z.ext, z.rows, z.layers
    first_row = lax.axis_index("lat") * rows - halo

    for e in range(ext):
        if first:
            zero = jnp.zeros((layers, z.cols), jnp.float32)
            a, p, q = zero, zero, zero
        elif e < halo:
            a, p, q = (above_in[c * halo + e] for c in range(3))
        elif e < halo + rows:
            a, p, q = (main_in[c * rows + e - halo] for c in range(3))
        else:
            a, p, q = (below_in[c * halo + e - halo - rows] for c in range(3))
        x_ref[e] = a + obs_ref[e]
        x_ref[ext + e] = p
        x_ref[2 * ext + e] = q

    mixers = [mix_ref[j * layers : (j + 1) * layers, :] for j in range(layers)]

    def run(j):
        order, stage = divmod(j, STAGES)
        source = (x_ref, y_ref, w_ref)[stage]
        target = (y_ref, w_ref, x_ref)[stage]
        low, high = j + 1, ext - j - 1

        def weighted(e, value):
            return h_ref[j * ext + e] * value

        def body(e, carry, place=None):
            b_before, b_here, a_here, q_before, q_here = carry
            a_after, q_after = source[e + 1], source[2 * ext + e + 1]
            b_after = weighted(e + 1, a_after)
            p_here = source[ext + e]
            oc, keep = oc_ref[e], keep_ref[e]
            coriolis = 2.0 * (0.3 + 0.4 * ((first_row + e).astype(jnp.float32) * (1.0 / total_rows) - 0.5))
            divergence = (
                pltpu.roll(p_here, z.cols - 1, axis=1) - pltpu.roll(p_here, 1, axis=1) + (q_after - q_before)
            )
            mixed = mixers[0] * divergence
            for k in range(1, layers):
                mixed = mixed + mixers[k] * pltpu.roll(divergence, k, axis=0)
            east = pltpu.roll(b_here, z.cols - 1, axis=1) - pltpu.roll(b_here, 1, axis=1)
            a = keep * a_here + oc * mixed
            p = keep * p_here + oc * (east + coriolis * q_here)
            q = keep * q_here + oc * (b_after - b_before - coriolis * p_here)
            if stage == 1:
                a = 0.75 * x_ref[e] + 0.25 * a
                p = 0.75 * x_ref[ext + e] + 0.25 * p
                q = 0.75 * x_ref[2 * ext + e] + 0.25 * q
            elif stage == 2:
                a = THIRD * x_ref[e] + TWO_THIRDS * a
                p = THIRD * x_ref[ext + e] + TWO_THIRDS * p
                q = THIRD * x_ref[2 * ext + e] + TWO_THIRDS * q
                if place is not None:
                    part = STEP_DT * a
                    if order > 0:
                        part = part + sum_ref[place]
                    if order < z.steps - 1:
                        sum_ref[place] = part
                    else:
                        bias_ref[place] = part
                        for c, value in enumerate((a, p, q)):
                            main_ref[c * rows + place] = value
                if order < z.steps - 1:
                    a = a + obs_ref[(order + 1) * ext + e]
            if not (stage == 2 and order == z.steps - 1):
                target[e] = a
                target[ext + e] = p
                target[2 * ext + e] = q
            return b_here, b_after, a_after, q_here, q_after

        a_first = source[low]
        carry = (
            weighted(low - 1, source[low - 1]),
            weighted(low, a_first),
            a_first,
            source[2 * ext + low - 1],
            source[2 * ext + low],
        )
        if stage < 2:
            over_rows(low, high, carry, body)
        else:
            carry = over_rows(low, halo, carry, body)
            carry = over_rows(0, rows, carry, lambda r, c: body(halo + r, c, place=r))
            over_rows(halo + rows, high, carry, body)

    for j in range(halo):
        run(j)
    for c in range(3):
        for m in range(halo):
            top_ref[c * halo + m] = main_ref[c * rows + m]
            bottom_ref[c * halo + m] = main_ref[c * rows + rows - halo + m]


def turn_kernel(z, count, lines_ref, out_ref):
    for c in range(count):
        layers_first(z, out_ref, c * z.layers * z.rows, [lines_ref[c * z.rows + r] for r in range(z.rows)])


def call(kernel, out_shapes, in_specs, scratch=(), cost=0):
    return pl.pallas_call(
        kernel,
        out_shape=[jax.ShapeDtypeStruct(s, jnp.float32) for s in out_shapes],
        in_specs=in_specs,
        out_specs=[VMEM] * len(out_shapes),
        scratch_shapes=list(scratch),
        compiler_params=pltpu.CompilerParams(vmem_limit_bytes=24 << 20),
        cost_estimate=pl.CostEstimate(flops=cost, bytes_accessed=4 << 20, transcendentals=0),
    )


def per_device(thickness, obs_cells, obs_values, ocean_mask, coupling, damping):
    _, steps, stages, layers, rows, cols = thickness.shape
    z = Sizes(steps, layers, rows, cols)
    n_win, n_lat = lax.axis_size("win"), lax.axis_size("lat")
    win = lax.axis_index("win")
    flat = thickness.reshape(steps * stages * layers * rows, cols)
    cube = (layers, cols)

    to_above, to_below, own = call(
        functools.partial(pack_kernel, z),
        [(z.packed,) + cube, (z.packed,) + cube, ((steps + 1) * rows, cols)],
        [VMEM] * 4,
    )(flat, obs_cells[0], obs_values[0], ocean_mask)
    southward = [(i, i + 1) for i in range(n_lat - 1)]
    northward = [(i + 1, i) for i in range(n_lat - 1)]
    above = lax.ppermute(to_below, "lat", southward)
    below = lax.ppermute(to_above, "lat", northward)
    fields = call(
        functools.partial(extend_kernel, z),
        [
            (z.halo * z.ext,) + cube,
            (steps * z.ext,) + cube,
            (z.ext,) + cube,
            (z.ext,) + cube,
            (layers * layers, cols),
        ],
        [SMEM, SMEM] + [VMEM] * 4,
    )(coupling, damping, flat, above, below, own)

    def relay(value, source_win, shift):
        pairs = [
            (source_win * n_lat + i, (source_win - 1) * n_lat + i + shift)
            for i in range(n_lat)
            if 0 <= i + shift < n_lat
        ]
        return lax.ppermute(value, ("win", "lat"), pairs)

    arrived = ()
    lam = bias = None
    total = None
    for source_win in reversed(range(n_win)):
        outs = call(
            functools.partial(window_kernel, z, n_lat * rows, not arrived),
            [
                (rows,) + cube,
                (3 * rows,) + cube,
                (3 * z.halo,) + cube,
                (3 * z.halo,) + cube,
            ],
            [VMEM] * (5 + len(arrived)),
            [pltpu.VMEM((3 * z.ext,) + cube, jnp.float32)] * 3 + [pltpu.VMEM((rows,) + cube, jnp.float32)],
            cost=40_000_000,
        )(*fields, *arrived)
        bias_here, main, top, bottom = outs
        lam = main if lam is None else jnp.where(win == source_win, main, lam)
        total = bias_here if total is None else total + bias_here
        if source_win:
            arrived = (
                relay(main, source_win, 0),
                relay(bottom, source_win, 1),
                relay(top, source_win, -1),
            )
            total = relay(total, source_win, 0)
    parts = [lax.ppermute(total, "win", [(0, w)]) for w in range(1, n_win)]
    result = jnp.where(win == 0, total, 0.0)
    for part in parts:
        result = result + part
    (lam,) = call(functools.partial(turn_kernel, z, 3), [(3 * layers * rows, cols)], [VMEM])(lam)
    (result,) = call(functools.partial(turn_kernel, z, 1), [(layers * rows, cols)], [VMEM])(result)
    return lam.reshape(1, 3, layers, rows, cols), result.reshape(layers, rows, cols)


def solution(mesh):
    in_specs = (
        P(("groups", "win"), None, None, None, "lat", None),
        P(("groups", "win"), None, "lat"),
        P(("groups", "win"), None, "lat"),
        P(("groups", "lat"), None),
        P(),
        P(),
    )
    out_specs = (P(("groups", "win"), None, None, "lat", None), P("groups", "lat", None))
    return jax.shard_map(
        per_device, mesh=mesh, in_specs=in_specs, out_specs=out_specs, check_vma=False
    )
```

```python
import functools

import jax
import jax.numpy as jnp
from jax import lax
from jax.experimental import pallas as pl
from jax.experimental.pallas import tpu as pltpu
from jax.sharding import PartitionSpec as P

STEP_DT = 0.2
THIRD = 1.0 / 3.0
TWO_THIRDS = 2.0 / 3.0
STAGES = 3
WEIGHTS = (1.0, 0.25, TWO_THIRDS)
SUBLANES = 8
LANES = 128

VMEM = pl.BlockSpec(memory_space=pltpu.VMEM)
HBM = pl.BlockSpec(memory_space=pltpu.HBM)
SMEM = pl.BlockSpec(memory_space=pltpu.SMEM)


class Sizes:
    def __init__(self, steps, layers, rows, cols):
        self.steps, self.layers, self.rows, self.cols = steps, layers, rows, cols
        self.halo = STAGES * steps
        self.ext = rows + 2 * self.halo
        self.first = [sum(self.halo - m for m in range(j)) for j in range(self.halo)]
        self.halo_rows = sum(self.halo - m for m in range(self.halo))
        self.tiles = rows // SUBLANES
        self.tail = -(-(steps + 1) * self.halo // SUBLANES)
        self.packed = self.halo_rows + self.tail
        self.fields = self.halo * rows + (steps + 1) * self.tiles

    def section(self, j):
        step, stage = self.steps - 1 - j // STAGES, j % STAGES
        return (step * STAGES + stage) * self.layers * self.rows


def rows_first(z, ref, base):
    lines = []
    for tile in range(z.rows // SUBLANES):
        block = jnp.stack(
            [ref[base + l * z.rows + tile * SUBLANES : base + l * z.rows + (tile + 1) * SUBLANES, :] for l in range(z.layers)]
        )
        block = jnp.swapaxes(block, 0, 1)
        lines.extend(block[m] for m in range(SUBLANES))
    return lines


def layers_first(z, ref, start, lines):
    for tile in range(z.rows // SUBLANES):
        block = jnp.swapaxes(jnp.stack(lines[tile * SUBLANES : (tile + 1) * SUBLANES]), 0, 1)
        for l in range(z.layers):
            low = start + l * z.rows + tile * SUBLANES
            ref[low : low + SUBLANES, :] = block[l]


def pack_kernel(z, th_in, cells_in, values_in, mask_in, up_ref, down_ref, own_ref, th_ref, cells_ref, values_ref, mask_ref, sem):
    copies = [
        pltpu.make_async_copy(source, target, sem.at[i])
        for i, (source, target) in enumerate(
            ((cells_in, cells_ref), (values_in, values_ref), (mask_in, mask_ref), (th_in, th_ref))
        )
    ]
    for copy in copies:
        copy.start()
    for copy in copies[:3]:
        copy.wait()
    count = cells_ref.shape[1]
    row_ids = lax.broadcasted_iota(jnp.int32, (z.rows, count), 0)
    col_ids = lax.broadcasted_iota(jnp.int32, (z.cols, count), 0)
    for order in range(z.steps):
        step = z.steps - 1 - order
        cells = cells_ref[step : step + 1, :]
        values = values_ref[step : step + 1, :]
        by_row = jnp.where(row_ids == cells // z.cols, values, 0.0)
        by_col = jnp.where(col_ids == cells % z.cols, 1.0, 0.0).astype(jnp.bfloat16)
        field = jnp.zeros((z.rows, z.cols), jnp.float32)
        for _ in range(3):
            part = by_row.astype(jnp.bfloat16)
            by_row = by_row - part.astype(jnp.float32)
            field = field + lax.dot_general(
                part, by_col, (((1,), (1,)), ((), ())), preferred_element_type=jnp.float32
            )
        own_ref[order * z.tiles : (order + 1) * z.tiles] = field.reshape(z.tiles, SUBLANES, z.cols)
    ocean = mask_ref[...].astype(jnp.float32) * (0.5 * STEP_DT)
    own_ref[z.steps * z.tiles :] = ocean.reshape(z.tiles, SUBLANES, z.cols)
    copies[3].wait()
    for j in range(z.halo):
        lines, need = rows_first(z, th_ref, z.section(j)), z.halo - j
        for m in range(need):
            up_ref[z.first[j] + m] = lines[m]
            down_ref[z.first[j] + m] = lines[z.rows - need + m]
    for k in range(z.steps + 1):
        for m in range(z.halo):
            tile, line = divmod(k * z.halo + m, SUBLANES)
            for ref, row in ((up_ref, m), (down_ref, z.rows - z.halo + m)):
                from_tile, from_line = divmod(k * z.rows + row, SUBLANES)
                ref[z.halo_rows + tile, line : line + 1, :] = own_ref[from_tile, from_line : from_line + 1, :]
    for q in range((z.steps + 1) * z.halo, z.tail * SUBLANES):
        tile, line = divmod(q, SUBLANES)
        for ref in (up_ref, down_ref):
            ref[z.halo_rows + tile, line : line + 1, :] = jnp.zeros((1, z.cols), jnp.float32)


def own_kernel(z, coupling_ref, damping_ref, th_ref, own_ref, h_ref, oc_ref, keep_ref, mix_ref):
    layer_ids = lax.broadcasted_iota(jnp.int32, (z.layers, LANES), 0)
    half = z.layers // 2
    for j in range(z.layers):
        line = jnp.zeros((z.layers, LANES), jnp.float32)
        for l in range(z.layers):
            target = l if j < half else (l + half) % z.layers
            k = (target - j) % z.layers
            weight = coupling_ref[k, target] + (1.0 if k == target else 0.0)
            line = jnp.where(layer_ids == l, weight, line)
        mix_ref[j * z.layers : (j + 1) * z.layers, :] = line
    rate = jnp.zeros((z.layers, LANES), jnp.float32)
    for l in range(z.layers):
        rate = jnp.where(layer_ids == l, 2.0 * damping_ref[l], rate)
    mix_ref[z.layers * z.layers :, :] = rate
    rate = jnp.concatenate([rate] * (z.cols // LANES), axis=1)
    for r in range(z.rows):
        tile, line = divmod(z.steps * z.rows + r, SUBLANES)
        oc = jnp.broadcast_to(own_ref[tile, line : line + 1, :], (z.layers, z.cols))
        keep = 1.0 - oc * rate
        for stage, weight in enumerate(WEIGHTS):
            oc_ref[stage * z.rows + r] = weight * oc
            keep_ref[stage * z.rows + r] = weight * keep
    for j in range(z.halo):
        for r, line in enumerate(rows_first(z, th_ref, z.section(j))):
            h_ref[j * z.rows + r] = line
    h_ref[z.halo * z.rows :] = own_ref[...]


def window_kernel(z, total_rows, first, last, target_win, *refs):
    h_ref, above_ref, below_ref = refs[:3]
    refs = refs[3:]
    own_ref = h_ref.at[pl.ds(z.halo * z.rows, (z.steps + 1) * z.tiles)]
    oc_ref, keep_ref, mix_ref = refs[:3]
    state, refs = refs[3 : 3 if first else 6], refs[3 if first else 6 :]
    if not first:
        lam_in, bias_in, refs = refs[0], refs[1], refs[2:]
        mine = lax.axis_index("win") == target_win
    if last:
        (bias_ref, lam_ref), refs = refs[:2], refs[2:]
    else:
        (bias_ref, lam_ref, main_ref, top_ref, bottom_ref), refs = refs[:5], refs[5:]
    x_ref, y_ref, w_ref, sum_ref, oc_out, keep_out = refs
    halo, ext, rows, layers = z.halo, z.ext, z.rows, z.layers
    first_row = lax.axis_index("lat") * rows - halo
    parts = z.cols // LANES
    lanes = [slice(i * LANES, (i + 1) * LANES) for i in range(parts)]
    shape = (layers, LANES)
    lane_ids = lax.broadcasted_iota(jnp.int32, shape, 1)
    at_start, at_end = lane_ids == 0, lane_ids == LANES - 1
    mixers = [mix_ref[j * layers : (j + 1) * layers, :] for j in range(layers)]

    def read(ref, row):
        return [ref[row, :, lane] for lane in lanes]

    def write(ref, row, values):
        for lane, value in zip(lanes, values):
            ref[row, :, lane] = value

    def each(function, *values):
        return [function(*v) for v in zip(*values)]

    def line(k, e):
        if e < halo:
            ref, (tile, at) = above_ref, divmod(k * halo + e, SUBLANES)
            tile += z.halo_rows
        elif e >= halo + rows:
            ref, (tile, at) = below_ref, divmod(k * halo + e - halo - rows, SUBLANES)
            tile += z.halo_rows
        else:
            ref, (tile, at) = own_ref, divmod(k * rows + e - halo, SUBLANES)
        return [jnp.broadcast_to(ref[tile, at : at + 1, lane], shape) for lane in lanes]

    def add(x, y):
        return each(lambda u, v: u + v, x, y)

    def incoming(c, e):
        main_in, above_in, below_in = state
        if e < halo:
            return read(above_in, c * halo + e)
        if e >= halo + rows:
            return read(below_in, c * halo + e - halo - rows)
        return read(main_in, c * rows + e - halo)

    def east(values):
        out = []
        for i, value in enumerate(values):
            after = jnp.where(at_start, values[(i + 1) % parts], value)
            before = jnp.where(at_end, values[i - 1], value)
            out.append(pltpu.roll(after, LANES - 1, axis=1) - pltpu.roll(before, 1, axis=1))
        return out

    def mixed(value):
        half = layers // 2
        low, high = mixers[0] * value, mixers[half] * value
        for k in range(1, half):
            turned = pltpu.roll(value, k, axis=0)
            low = low + mixers[k] * turned
            high = high + mixers[half + k] * turned
        return low + pltpu.roll(high, half, axis=0)

    zero = [jnp.zeros(shape, jnp.float32)] * parts
    for e in range(ext):
        a, p, q = (zero, zero, zero) if first else (incoming(c, e) for c in range(3))
        write(x_ref, e, add(a, line(0, e)))
        write(x_ref, ext + e, p)
        write(x_ref, 2 * ext + e, q)
    rate = mix_ref[layers * layers :, :]
    for i in range(2 * halo):
        oc = line(z.steps, i if i < halo else rows + i)
        keep = each(lambda v: 1.0 - v * rate, oc)
        for stage, weight in enumerate(WEIGHTS):
            write(oc_out, stage * 2 * halo + i, each(lambda v: weight * v, oc))
            write(keep_out, stage * 2 * halo + i, each(lambda v: weight * v, keep))

    def factors(stage, e):
        if halo <= e < halo + rows:
            return (read(ref, stage * rows + e - halo) for ref in (oc_ref, keep_ref))
        i = e if e < halo else e - rows
        return (read(ref, stage * 2 * halo + i) for ref in (oc_out, keep_out))

    def thickness(j, e):
        if e < halo:
            return read(above_ref, z.first[j] + e - j)
        if e >= halo + rows:
            return read(below_ref, z.first[j] + e - halo - rows)
        return read(h_ref, j * rows + e - halo)

    def run(j):
        order, stage = divmod(j, STAGES)
        source = (x_ref, y_ref, w_ref)[stage]
        target = (y_ref, w_ref, x_ref)[stage]
        low, high = j + 1, ext - j - 1

        def weighted(e, values):
            return each(lambda h, v: h * v, thickness(j, e), values)

        def body(e, carry):
            place = e - halo if halo <= e < halo + rows else None
            b_before, b_here, a_here, q_before, q_here = carry
            a_after, q_after = read(source, e + 1), read(source, 2 * ext + e + 1)
            b_after = weighted(e + 1, a_after)
            p_here = read(source, ext + e)
            oc, keep = factors(stage, e)
            row = jnp.asarray(first_row + e).astype(jnp.float32)
            coriolis = 2.0 * (0.3 + 0.4 * (row * (1.0 / total_rows) - 0.5))
            divergence = each(lambda x, n, s: x + (n - s), east(p_here), q_after, q_before)
            a = each(lambda k, v, o, m: k * v + o * mixed(m), keep, a_here, oc, divergence)
            p = each(lambda k, v, o, d, u: k * v + o * (d + coriolis * u), keep, p_here, oc, east(b_here), q_here)
            q = each(
                lambda k, v, o, n, s, u: k * v + o * ((n - s) - coriolis * u),
                keep, q_here, oc, b_after, b_before, p_here,
            )
            if stage:
                rest = 1.0 - WEIGHTS[stage]
                start = [read(x_ref, c * ext + e) for c in range(3)]
                a, p, q = (each(lambda s, v: rest * s + v, start[c], v) for c, v in enumerate((a, p, q)))
            if stage == STAGES - 1:
                if place is not None:
                    part = each(lambda v: STEP_DT * v, a)
                    if order > 0:
                        part = add(part, read(sum_ref, place))
                    if order < z.steps - 1:
                        write(sum_ref, place, part)
                    else:
                        if not first:
                            part = each(lambda v, o: jnp.where(mine, v, o), part, read(bias_in, place))
                        write(bias_ref, place, part)
                    if order == z.steps - 1:
                        for c, value in enumerate((a, p, q)):
                            if not last:
                                write(main_ref, c * rows + place, value)
                            if not first:
                                old = read(lam_in, c * rows + place)
                                value = each(lambda v, o: jnp.where(mine, v, o), value, old)
                            write(lam_ref, c * rows + place, value)
                if order < z.steps - 1:
                    a = add(a, line(order + 1, e))
            if j < halo - 1:
                for c, value in enumerate((a, p, q)):
                    write(target, c * ext + e, value)
            return b_here, b_after, a_after, q_here, q_after

        a_first = read(source, low)
        carry = (
            weighted(low - 1, read(source, low - 1)),
            weighted(low, a_first),
            a_first,
            read(source, 2 * ext + low - 1),
            read(source, 2 * ext + low),
        )
        for e in range(low, high):
            carry = body(e, carry)

    for j in range(halo):
        run(j)
    if not last:
        for c in range(3):
            for m in range(halo):
                top_ref[c * halo + m] = main_ref[c * rows + m]
                bottom_ref[c * halo + m] = main_ref[c * rows + rows - halo + m]


def turn_kernel(z, count, lines_ref, out_ref):
    for c in range(count):
        layers_first(z, out_ref, c * z.layers * z.rows, [lines_ref[c * z.rows + r] for r in range(z.rows)])


def call(kernel, out_shapes, in_specs, scratch=(), cost=0, limit=8 << 20, space=pltpu.VMEM):
    return pl.pallas_call(
        kernel,
        out_shape=[space(s, jnp.float32) for s in out_shapes],
        in_specs=in_specs,
        out_specs=[VMEM] * len(out_shapes),
        scratch_shapes=list(scratch),
        compiler_params=pltpu.CompilerParams(vmem_limit_bytes=limit),
        cost_estimate=pl.CostEstimate(flops=cost, bytes_accessed=4 << 20, transcendentals=0),
    )


def window_scratch(z):
    counts = [3 * z.ext] * 3 + [z.rows] + [STAGES * 2 * z.halo] * 2
    return [pltpu.VMEM((count, z.layers, z.cols), jnp.float32) for count in counts]


def per_device(thickness, obs_cells, obs_values, ocean_mask, coupling, damping):
    _, steps, stages, layers, rows, cols = thickness.shape
    z = Sizes(steps, layers, rows, cols)
    n_win, n_lat = lax.axis_size("win"), lax.axis_size("lat")
    win = lax.axis_index("win")
    flat = thickness.reshape(steps * stages * layers * rows, cols)
    cube = (layers, cols)
    count = obs_cells.shape[2]

    to_above, to_below, own = call(
        functools.partial(pack_kernel, z),
        [(z.packed,) + cube, (z.packed,) + cube, ((steps + 1) * z.tiles,) + cube],
        [HBM] * 4,
        [
            pltpu.VMEM(flat.shape, jnp.float32),
            pltpu.VMEM((steps, count), jnp.int32),
            pltpu.VMEM((steps, count), jnp.float32),
            pltpu.VMEM((rows, cols), jnp.int32),
            pltpu.SemaphoreType.DMA((4,)),
        ],
        limit=60 << 20,
    )(flat, obs_cells[0], obs_values[0], ocean_mask)
    southward = [(i, i + 1) for i in range(n_lat - 1)]
    northward = [(i + 1, i) for i in range(n_lat - 1)]
    above = lax.ppermute(to_below, "lat", southward)
    below = lax.ppermute(to_above, "lat", northward)
    h, *tables = call(
        functools.partial(own_kernel, z),
        [
            (z.fields,) + cube,
            (STAGES * rows,) + cube,
            (STAGES * rows,) + cube,
            ((layers + 1) * layers, LANES),
        ],
        [SMEM, SMEM, VMEM, VMEM],
    )(coupling, damping, flat, own)

    def relay(value, source_win, target_win, shift=0):
        pairs = [
            (source_win * n_lat + i, target_win * n_lat + i + shift)
            for i in range(n_lat)
            if 0 <= i + shift < n_lat
        ]
        return lax.ppermute(value, ("win", "lat"), pairs)

    fields = (h, above, below, *tables)
    one, state_rows, halo_rows = ((n,) + cube for n in (rows, 3 * rows, 3 * z.halo))

    def window(target_win, state, results):
        last = target_win == 0
        outs = [one, state_rows] if last else [one, state_rows, state_rows, halo_rows, halo_rows]
        operands = fields + state + results
        return call(
            functools.partial(window_kernel, z, n_lat * rows, not state, last, target_win),
            outs,
            [VMEM] * len(operands),
            window_scratch(z),
            cost=40_000_000,
        )(*operands)

    bias, lam, main, top, bottom = window(n_win - 1, (), ())
    for source_win in range(n_win - 1, 0, -1):
        state = (
            relay(main, source_win, source_win - 1),
            relay(bottom, source_win, source_win - 1, 1),
            relay(top, source_win, source_win - 1, -1),
        )
        if source_win > 1:
            bias, lam, main, top, bottom = window(source_win - 1, state, (lam, bias))
    others = n_win - 1
    for shift in range(1, others):
        pairs = [
            ((1 + w) * n_lat + i, (1 + (w + shift) % others) * n_lat + i) for w in range(others) for i in range(n_lat)
        ]
        part = lax.ppermute(bias, ("win", "lat"), pairs)
        total = part if shift == 1 else total + part
    total = bias if others == 1 else bias + total
    mine, lam = window(0, state, (lam, total))
    swap = [(a * n_lat + i, (1 - a) * n_lat + i) for a in range(2) for i in range(n_lat)]
    result = mine + sum(relay(mine, 0, target_win) for target_win in range(n_win - 1, 1, -1))
    result = result + lax.ppermute(mine, ("win", "lat"), swap)
    (lam,) = call(functools.partial(turn_kernel, z, 3), [(3 * layers * rows, cols)], [VMEM], space=jax.ShapeDtypeStruct)(lam)
    (result,) = call(functools.partial(turn_kernel, z, 1), [(layers * rows, cols)], [VMEM], space=jax.ShapeDtypeStruct)(result)
    return lam.reshape(1, 3, layers, rows, cols), result.reshape(layers, rows, cols)


def solution(mesh):
    in_specs = (
        P(("groups", "win"), None, None, None, "lat", None),
        P(("groups", "win"), None, "lat"),
        P(("groups", "win"), None, "lat"),
        P(("groups", "lat"), None),
        P(),
        P(),
    )
    out_specs = (P(("groups", "win"), None, None, "lat", None), P("groups", "lat", None))
    return jax.shard_map(
        per_device, mesh=mesh, in_specs=in_specs, out_specs=out_specs, check_vma=False
    )
```

```python
import functools

import jax
import jax.numpy as jnp
from jax import lax
from jax.experimental import pallas as pl
from jax.experimental.pallas import tpu as pltpu
from jax.sharding import PartitionSpec as P

STEP_DT = 0.2
THIRD = 1.0 / 3.0
TWO_THIRDS = 2.0 / 3.0
STAGES = 3
WEIGHTS = (1.0, 0.25, TWO_THIRDS)
SUBLANES = 8
LANES = 128

VMEM = pl.BlockSpec(memory_space=pltpu.VMEM)
HBM = pl.BlockSpec(memory_space=pltpu.HBM)
SMEM = pl.BlockSpec(memory_space=pltpu.SMEM)


class Sizes:
    def __init__(self, steps, layers, rows, cols):
        self.steps, self.layers, self.rows, self.cols = steps, layers, rows, cols
        self.halo = STAGES * steps
        self.ext = rows + 2 * self.halo
        self.first = [sum(self.halo - m for m in range(j)) for j in range(self.halo)]
        self.halo_rows = sum(self.halo - m for m in range(self.halo))
        self.tiles = rows // SUBLANES
        self.tail = -(-(steps + 1) * self.halo // SUBLANES)
        self.packed = self.halo_rows + self.tail
        self.fields = self.halo * rows + (steps + 1) * self.tiles

    def section(self, j):
        step, stage = self.steps - 1 - j // STAGES, j % STAGES
        return (step * STAGES + stage) * self.layers * self.rows


def rows_first(z, ref, base):
    lines = []
    for tile in range(z.rows // SUBLANES):
        block = jnp.stack(
            [ref[base + l * z.rows + tile * SUBLANES : base + l * z.rows + (tile + 1) * SUBLANES, :] for l in range(z.layers)]
        )
        block = jnp.swapaxes(block, 0, 1)
        lines.extend(block[m] for m in range(SUBLANES))
    return lines


def layers_first(z, ref, start, lines):
    for tile in range(z.rows // SUBLANES):
        block = jnp.swapaxes(jnp.stack(lines[tile * SUBLANES : (tile + 1) * SUBLANES]), 0, 1)
        for l in range(z.layers):
            low = start + l * z.rows + tile * SUBLANES
            ref[low : low + SUBLANES, :] = block[l]


def pack_kernel(z, th_in, cells_in, values_in, mask_in, partner_ref, other_ref, own_ref, th_ref, cells_ref, values_ref, mask_ref, sem):
    copies = [
        pltpu.make_async_copy(source, target, sem.at[i])
        for i, (source, target) in enumerate(
            ((cells_in, cells_ref), (values_in, values_ref), (mask_in, mask_ref), (th_in, th_ref))
        )
    ]
    for copy in copies:
        copy.start()
    for copy in copies[:3]:
        copy.wait()
    count = cells_ref.shape[1]
    row_ids = lax.broadcasted_iota(jnp.int32, (z.rows, count), 0)
    col_ids = lax.broadcasted_iota(jnp.int32, (z.cols, count), 0)
    for order in range(z.steps):
        step = z.steps - 1 - order
        cells = cells_ref[step : step + 1, :]
        values = values_ref[step : step + 1, :]
        by_row = jnp.where(row_ids == cells // z.cols, values, 0.0)
        by_col = jnp.where(col_ids == cells % z.cols, 1.0, 0.0).astype(jnp.bfloat16)
        field = jnp.zeros((z.rows, z.cols), jnp.float32)
        for _ in range(3):
            part = by_row.astype(jnp.bfloat16)
            by_row = by_row - part.astype(jnp.float32)
            field = field + lax.dot_general(
                part, by_col, (((1,), (1,)), ((), ())), preferred_element_type=jnp.float32
            )
        own_ref[order * z.tiles : (order + 1) * z.tiles] = field.reshape(z.tiles, SUBLANES, z.cols)
    ocean = mask_ref[...].astype(jnp.float32) * (0.5 * STEP_DT)
    own_ref[z.steps * z.tiles :] = ocean.reshape(z.tiles, SUBLANES, z.cols)
    copies[3].wait()
    even = lax.axis_index("lat") % 2 == 0
    for j in range(z.halo):
        lines, need = rows_first(z, th_ref, z.section(j)), z.halo - j
        for m in range(need):
            head, foot = lines[m], lines[z.rows - need + m]
            partner_ref[z.first[j] + m] = jnp.where(even, foot, head)
            other_ref[z.first[j] + m] = jnp.where(even, head, foot)
    for q in range(z.tail * SUBLANES):
        tile, line = divmod(q, SUBLANES)
        k, m = divmod(q, z.halo)
        head = foot = jnp.zeros((1, z.cols), jnp.float32)
        if k <= z.steps:
            places = (divmod(k * z.rows + row, SUBLANES) for row in (m, z.rows - z.halo + m))
            head, foot = (own_ref[t, at : at + 1, :] for t, at in places)
        partner_ref[z.halo_rows + tile, line : line + 1, :] = jnp.where(even, foot, head)
        other_ref[z.halo_rows + tile, line : line + 1, :] = jnp.where(even, head, foot)


def own_kernel(z, coupling_ref, damping_ref, th_ref, own_ref, h_ref, oc_ref, keep_ref, mix_ref):
    layer_ids = lax.broadcasted_iota(jnp.int32, (z.layers, LANES), 0)
    half = z.layers // 2
    for j in range(z.layers):
        line = jnp.zeros((z.layers, LANES), jnp.float32)
        for l in range(z.layers):
            target = l if j < half else (l + half) % z.layers
            k = (target - j) % z.layers
            weight = coupling_ref[k, target] + (1.0 if k == target else 0.0)
            line = jnp.where(layer_ids == l, weight, line)
        mix_ref[j * z.layers : (j + 1) * z.layers, :] = line
    rate = jnp.zeros((z.layers, LANES), jnp.float32)
    for l in range(z.layers):
        rate = jnp.where(layer_ids == l, 2.0 * damping_ref[l], rate)
    mix_ref[z.layers * z.layers :, :] = rate
    rate = jnp.concatenate([rate] * (z.cols // LANES), axis=1)
    for r in range(z.rows):
        tile, line = divmod(z.steps * z.rows + r, SUBLANES)
        oc = jnp.broadcast_to(own_ref[tile, line : line + 1, :], (z.layers, z.cols))
        keep = 1.0 - oc * rate
        for stage, weight in enumerate(WEIGHTS):
            oc_ref[stage * z.rows + r] = weight * oc
            keep_ref[stage * z.rows + r] = weight * keep
    for j in range(z.halo):
        for r, line in enumerate(rows_first(z, th_ref, z.section(j))):
            h_ref[j * z.rows + r] = line
    h_ref[z.halo * z.rows :] = own_ref[...]


def window_kernel(z, total_rows, first, last, target_win, *refs):
    even = lax.axis_index("lat") % 2 == 0
    h_ref, above_ref, below_ref = refs[:3]
    refs = refs[3:]
    if first:
        partner_ref, other_ref = above_ref, below_ref
        above_ref, below_ref = refs[3:5]
        refs = refs[:3] + refs[5:]
        for m in range(z.packed):
            above_ref[m] = jnp.where(even, other_ref[m], partner_ref[m])
            below_ref[m] = jnp.where(even, partner_ref[m], other_ref[m])
    own_ref = h_ref.at[pl.ds(z.halo * z.rows, (z.steps + 1) * z.tiles)]
    oc_ref, keep_ref, mix_ref = refs[:3]
    state, refs = refs[3 : 3 if first else 6], refs[3 if first else 6 :]
    if not first:
        lam_in, bias_in, refs = refs[0], refs[1], refs[2:]
        mine = lax.axis_index("win") == target_win
    if last:
        (bias_ref, lam_ref), refs = refs[:2], refs[2:]
    else:
        (bias_ref, lam_ref, main_ref, partner_out, other_out), refs = refs[:5], refs[5:]
    x_ref, y_ref, w_ref, sum_ref, oc_out, keep_out = refs
    halo, ext, rows, layers = z.halo, z.ext, z.rows, z.layers
    first_row = lax.axis_index("lat") * rows - halo
    parts = z.cols // LANES
    lanes = [slice(i * LANES, (i + 1) * LANES) for i in range(parts)]
    shape = (layers, LANES)
    lane_ids = lax.broadcasted_iota(jnp.int32, shape, 1)
    at_start, at_end = lane_ids == 0, lane_ids == LANES - 1
    mixers = [mix_ref[j * layers : (j + 1) * layers, :] for j in range(layers)]

    def read(ref, row):
        return [ref[row, :, lane] for lane in lanes]

    def write(ref, row, values):
        for lane, value in zip(lanes, values):
            ref[row, :, lane] = value

    def each(function, *values):
        return [function(*v) for v in zip(*values)]

    def line(k, e):
        if e < halo:
            ref, (tile, at) = above_ref, divmod(k * halo + e, SUBLANES)
            tile += z.halo_rows
        elif e >= halo + rows:
            ref, (tile, at) = below_ref, divmod(k * halo + e - halo - rows, SUBLANES)
            tile += z.halo_rows
        else:
            ref, (tile, at) = own_ref, divmod(k * rows + e - halo, SUBLANES)
        return [jnp.broadcast_to(ref[tile, at : at + 1, lane], shape) for lane in lanes]

    def add(x, y):
        return each(lambda u, v: u + v, x, y)

    def incoming(c, e):
        main_in, partner_in, other_in = state
        if not halo <= e < halo + rows:
            m = c * halo + (e if e < halo else e - halo - rows)
            pair, rest = read(partner_in, m), read(other_in, m)
            swap = even if e < halo else jnp.logical_not(even)
            return each(lambda u, v: jnp.where(swap, v, u), pair, rest)
        return read(main_in, c * rows + e - halo)

    def east(values):
        out = []
        for i, value in enumerate(values):
            after = jnp.where(at_start, values[(i + 1) % parts], value)
            before = jnp.where(at_end, values[i - 1], value)
            out.append(pltpu.roll(after, LANES - 1, axis=1) - pltpu.roll(before, 1, axis=1))
        return out

    def mixed(value):
        half = layers // 2
        low, high = mixers[0] * value, mixers[half] * value
        for k in range(1, half):
            turned = pltpu.roll(value, k, axis=0)
            low = low + mixers[k] * turned
            high = high + mixers[half + k] * turned
        return low + pltpu.roll(high, half, axis=0)

    zero = [jnp.zeros(shape, jnp.float32)] * parts
    for e in range(ext):
        a, p, q = (zero, zero, zero) if first else (incoming(c, e) for c in range(3))
        write(x_ref, e, add(a, line(0, e)))
        write(x_ref, ext + e, p)
        write(x_ref, 2 * ext + e, q)
    rate = mix_ref[layers * layers :, :]
    for i in range(2 * halo):
        oc = line(z.steps, i if i < halo else rows + i)
        keep = each(lambda v: 1.0 - v * rate, oc)
        for stage, weight in enumerate(WEIGHTS):
            write(oc_out, stage * 2 * halo + i, each(lambda v: weight * v, oc))
            write(keep_out, stage * 2 * halo + i, each(lambda v: weight * v, keep))

    def factors(stage, e):
        if halo <= e < halo + rows:
            return (read(ref, stage * rows + e - halo) for ref in (oc_ref, keep_ref))
        i = e if e < halo else e - rows
        return (read(ref, stage * 2 * halo + i) for ref in (oc_out, keep_out))

    def thickness(j, e):
        if e < halo:
            return read(above_ref, z.first[j] + e - j)
        if e >= halo + rows:
            return read(below_ref, z.first[j] + e - halo - rows)
        return read(h_ref, j * rows + e - halo)

    def run(j):
        order, stage = divmod(j, STAGES)
        source = (x_ref, y_ref, w_ref)[stage]
        target = (y_ref, w_ref, x_ref)[stage]
        low, high = j + 1, ext - j - 1

        def weighted(e, values):
            return each(lambda h, v: h * v, thickness(j, e), values)

        def body(e, carry):
            place = e - halo if halo <= e < halo + rows else None
            b_before, b_here, a_here, q_before, q_here = carry
            a_after, q_after = read(source, e + 1), read(source, 2 * ext + e + 1)
            b_after = weighted(e + 1, a_after)
            p_here = read(source, ext + e)
            oc, keep = factors(stage, e)
            row = jnp.asarray(first_row + e).astype(jnp.float32)
            coriolis = 2.0 * (0.3 + 0.4 * (row * (1.0 / total_rows) - 0.5))
            divergence = each(lambda x, n, s: x + (n - s), east(p_here), q_after, q_before)
            a = each(lambda k, v, o, m: k * v + o * mixed(m), keep, a_here, oc, divergence)
            p = each(lambda k, v, o, d, u: k * v + o * (d + coriolis * u), keep, p_here, oc, east(b_here), q_here)
            q = each(
                lambda k, v, o, n, s, u: k * v + o * ((n - s) - coriolis * u),
                keep, q_here, oc, b_after, b_before, p_here,
            )
            if stage:
                rest = 1.0 - WEIGHTS[stage]
                start = [read(x_ref, c * ext + e) for c in range(3)]
                a, p, q = (each(lambda s, v: rest * s + v, start[c], v) for c, v in enumerate((a, p, q)))
            if stage == STAGES - 1:
                if place is not None:
                    part = each(lambda v: STEP_DT * v, a)
                    if order > 0:
                        part = add(part, read(sum_ref, place))
                    if order < z.steps - 1:
                        write(sum_ref, place, part)
                    else:
                        if not first:
                            part = each(lambda v, o: jnp.where(mine, v, o), part, read(bias_in, place))
                        write(bias_ref, place, part)
                    if order == z.steps - 1:
                        for c, value in enumerate((a, p, q)):
                            if not last:
                                write(main_ref, c * rows + place, value)
                            if not first:
                                old = read(lam_in, c * rows + place)
                                value = each(lambda v, o: jnp.where(mine, v, o), value, old)
                            write(lam_ref, c * rows + place, value)
                if order < z.steps - 1:
                    a = add(a, line(order + 1, e))
            if j < halo - 1:
                for c, value in enumerate((a, p, q)):
                    write(target, c * ext + e, value)
            return b_here, b_after, a_after, q_here, q_after

        a_first = read(source, low)
        carry = (
            weighted(low - 1, read(source, low - 1)),
            weighted(low, a_first),
            a_first,
            read(source, 2 * ext + low - 1),
            read(source, 2 * ext + low),
        )
        for e in range(low, high):
            carry = body(e, carry)

    for j in range(halo):
        run(j)
    if not last:
        for c in range(3):
            for m in range(halo):
                head, foot = main_ref[c * rows + m], main_ref[c * rows + rows - halo + m]
                partner_out[c * halo + m] = jnp.where(even, foot, head)
                other_out[c * halo + m] = jnp.where(even, head, foot)


def turn_kernel(z, count, lines_ref, out_ref):
    for c in range(count):
        layers_first(z, out_ref, c * z.layers * z.rows, [lines_ref[c * z.rows + r] for r in range(z.rows)])


def call(kernel, out_shapes, in_specs, scratch=(), cost=0, limit=8 << 20, space=pltpu.VMEM):
    return pl.pallas_call(
        kernel,
        out_shape=[space(s, jnp.float32) for s in out_shapes],
        in_specs=in_specs,
        out_specs=[VMEM] * len(out_shapes),
        scratch_shapes=list(scratch),
        compiler_params=pltpu.CompilerParams(vmem_limit_bytes=limit),
        cost_estimate=pl.CostEstimate(flops=cost, bytes_accessed=4 << 20, transcendentals=0),
    )


def window_scratch(z):
    counts = [3 * z.ext] * 3 + [z.rows] + [STAGES * 2 * z.halo] * 2
    return [pltpu.VMEM((count, z.layers, z.cols), jnp.float32) for count in counts]


def per_device(thickness, obs_cells, obs_values, ocean_mask, coupling, damping):
    _, steps, stages, layers, rows, cols = thickness.shape
    z = Sizes(steps, layers, rows, cols)
    n_win, n_lat = lax.axis_size("win"), lax.axis_size("lat")
    win = lax.axis_index("win")
    flat = thickness.reshape(steps * stages * layers * rows, cols)
    cube = (layers, cols)
    count = obs_cells.shape[2]

    to_partner, to_other, own = call(
        functools.partial(pack_kernel, z),
        [(z.packed,) + cube, (z.packed,) + cube, ((steps + 1) * z.tiles,) + cube],
        [HBM] * 4,
        [
            pltpu.VMEM(flat.shape, jnp.float32),
            pltpu.VMEM((steps, count), jnp.int32),
            pltpu.VMEM((steps, count), jnp.float32),
            pltpu.VMEM((rows, cols), jnp.int32),
            pltpu.SemaphoreType.DMA((4,)),
        ],
        limit=60 << 20,
    )(flat, obs_cells[0], obs_values[0], ocean_mask)
    pairs, rests = ([(i + d, i + 1 - d) for i in range(k, n_lat - 1, 2) for d in range(2)] for k in range(2))
    near = (lax.ppermute(to_partner, "lat", pairs), lax.ppermute(to_other, "lat", rests))
    h, *tables = call(
        functools.partial(own_kernel, z),
        [
            (z.fields,) + cube,
            (STAGES * rows,) + cube,
            (STAGES * rows,) + cube,
            ((layers + 1) * layers, LANES),
        ],
        [SMEM, SMEM, VMEM, VMEM],
    )(coupling, damping, flat, own)

    straight = [(i, i) for i in range(n_lat)]

    def relay(value, source_win, target_win, among=straight):
        moves = [(source_win * n_lat + i, target_win * n_lat + j) for i, j in among]
        return lax.ppermute(value, ("win", "lat"), moves)

    one, state_rows, halo_rows = ((n,) + cube for n in (rows, 3 * rows, 3 * z.halo))

    def window(target_win, fields, state, results):
        first, last = target_win == n_win - 1, target_win == 0
        outs = [one, state_rows] if last else [one, state_rows, state_rows, halo_rows, halo_rows]
        operands = fields + tuple(tables) + state + results
        return call(
            functools.partial(window_kernel, z, n_lat * rows, first, last, target_win),
            ([(z.packed,) + cube] * 2 if first else []) + outs,
            [VMEM] * len(operands),
            window_scratch(z),
            cost=40_000_000,
        )(*operands)

    above, below, bias, lam, main, partner, other = window(n_win - 1, (h,) + near, (), ())
    fields = (h, above, below)
    for source_win in range(n_win - 1, 0, -1):
        state = (
            relay(main, source_win, source_win - 1),
            relay(partner, source_win, source_win - 1, pairs),
            relay(other, source_win, source_win - 1, rests),
        )
        if source_win > 1:
            bias, lam, main, partner, other = window(source_win - 1, fields, state, (lam, bias))
    others = n_win - 1
    total = bias
    for shift in range(1, others):
        moves = [
            ((1 + w) * n_lat + i, (1 + (w + shift) % others) * n_lat + i) for w in range(others) for i in range(n_lat)
        ]
        total = total + lax.ppermute(bias, ("win", "lat"), moves)
    mine, lam = window(0, fields, state, (lam, total))
    swap = [(a * n_lat + i, (1 - a) * n_lat + i) for a in range(2) for i in range(n_lat)]
    result = mine + sum(relay(mine, 0, target_win) for target_win in range(n_win - 1, 1, -1))
    result = result + lax.ppermute(mine, ("win", "lat"), swap)
    (lam,) = call(functools.partial(turn_kernel, z, 3), [(3 * layers * rows, cols)], [VMEM], space=jax.ShapeDtypeStruct)(lam)
    (result,) = call(functools.partial(turn_kernel, z, 1), [(layers * rows, cols)], [VMEM], space=jax.ShapeDtypeStruct)(result)
    return lam.reshape(1, 3, layers, rows, cols), result.reshape(layers, rows, cols)


def solution(mesh):
    in_specs = (
        P(("groups", "win"), None, None, None, "lat", None),
        P(("groups", "win"), None, "lat"),
        P(("groups", "win"), None, "lat"),
        P(("groups", "lat"), None),
        P(),
        P(),
    )
    out_specs = (P(("groups", "win"), None, None, "lat", None), P("groups", "lat", None))
    return jax.shard_map(
        per_device, mesh=mesh, in_specs=in_specs, out_specs=out_specs, check_vma=False
    )
```

```python
import functools

import jax
import jax.numpy as jnp
from jax import lax
from jax.experimental import pallas as pl
from jax.experimental.pallas import tpu as pltpu
from jax.sharding import PartitionSpec as P

STEP_DT = 0.2
THIRD = 1.0 / 3.0
TWO_THIRDS = 2.0 / 3.0
STAGES = 3
WEIGHTS = (1.0, 0.25, TWO_THIRDS)
SUBLANES = 8
LANES = 128

VMEM = pl.BlockSpec(memory_space=pltpu.VMEM)
HBM = pl.BlockSpec(memory_space=pltpu.HBM)
SMEM = pl.BlockSpec(memory_space=pltpu.SMEM)


class Sizes:
    def __init__(self, steps, layers, rows, cols):
        self.steps, self.layers, self.rows, self.cols = steps, layers, rows, cols
        self.halo = STAGES * steps
        self.ext = rows + 2 * self.halo
        self.first = [sum(self.halo - m for m in range(j)) for j in range(self.halo)]
        self.halo_rows = sum(self.halo - m for m in range(self.halo))
        self.tiles = rows // SUBLANES
        self.tail = -(-(steps + 1) * self.halo // SUBLANES)
        self.packed = self.halo_rows + self.tail
        self.fields = self.halo * rows + (steps + 1) * self.tiles

    def section(self, j):
        step, stage = self.steps - 1 - j // STAGES, j % STAGES
        return (step * STAGES + stage) * self.layers * self.rows


def rows_first(z, ref, base):
    lines = []
    for tile in range(z.rows // SUBLANES):
        block = jnp.stack(
            [ref[base + l * z.rows + tile * SUBLANES : base + l * z.rows + (tile + 1) * SUBLANES, :] for l in range(z.layers)]
        )
        block = jnp.swapaxes(block, 0, 1)
        lines.extend(block[m] for m in range(SUBLANES))
    return lines


def layers_first(z, ref, start, lines):
    for tile in range(z.rows // SUBLANES):
        block = jnp.swapaxes(jnp.stack(lines[tile * SUBLANES : (tile + 1) * SUBLANES]), 0, 1)
        for l in range(z.layers):
            low = start + l * z.rows + tile * SUBLANES
            ref[low : low + SUBLANES, :] = block[l]


def pack_kernel(z, th_in, cells_in, values_in, mask_in, partner_ref, other_ref, own_ref, th_ref, cells_ref, values_ref, mask_ref, sem):
    copies = [
        pltpu.make_async_copy(source, target, sem.at[i])
        for i, (source, target) in enumerate(
            ((cells_in, cells_ref), (values_in, values_ref), (mask_in, mask_ref), (th_in, th_ref))
        )
    ]
    for copy in copies:
        copy.start()
    for copy in copies[:3]:
        copy.wait()
    count = cells_ref.shape[1]
    row_ids = lax.broadcasted_iota(jnp.int32, (z.rows, count), 0)
    col_ids = lax.broadcasted_iota(jnp.int32, (z.cols, count), 0)
    for order in range(z.steps):
        step = z.steps - 1 - order
        cells = cells_ref[step : step + 1, :]
        values = values_ref[step : step + 1, :]
        by_row = jnp.where(row_ids == cells // z.cols, values, 0.0)
        by_col = jnp.where(col_ids == cells % z.cols, 1.0, 0.0).astype(jnp.bfloat16)
        field = jnp.zeros((z.rows, z.cols), jnp.float32)
        for _ in range(3):
            part = by_row.astype(jnp.bfloat16)
            by_row = by_row - part.astype(jnp.float32)
            field = field + lax.dot_general(
                part, by_col, (((1,), (1,)), ((), ())), preferred_element_type=jnp.float32
            )
        own_ref[order * z.tiles : (order + 1) * z.tiles] = field.reshape(z.tiles, SUBLANES, z.cols)
    ocean = mask_ref[...].astype(jnp.float32) * (0.5 * STEP_DT)
    own_ref[z.steps * z.tiles :] = ocean.reshape(z.tiles, SUBLANES, z.cols)
    copies[3].wait()
    even = lax.axis_index("lat") % 2 == 0
    for j in range(z.halo):
        lines, need = rows_first(z, th_ref, z.section(j)), z.halo - j
        for m in range(need):
            head, foot = lines[m], lines[z.rows - need + m]
            partner_ref[z.first[j] + m] = jnp.where(even, foot, head)
            other_ref[z.first[j] + m] = jnp.where(even, head, foot)
    for q in range(z.tail * SUBLANES):
        tile, line = divmod(q, SUBLANES)
        k, m = divmod(q, z.halo)
        head = foot = jnp.zeros((1, z.cols), jnp.float32)
        if k <= z.steps:
            places = (divmod(k * z.rows + row, SUBLANES) for row in (m, z.rows - z.halo + m))
            head, foot = (own_ref[t, at : at + 1, :] for t, at in places)
        partner_ref[z.halo_rows + tile, line : line + 1, :] = jnp.where(even, foot, head)
        other_ref[z.halo_rows + tile, line : line + 1, :] = jnp.where(even, head, foot)


def own_kernel(z, coupling_ref, damping_ref, th_ref, own_ref, h_ref, oc_ref, keep_ref, mix_ref):
    layer_ids = lax.broadcasted_iota(jnp.int32, (z.layers, LANES), 0)
    half = z.layers // 2
    for j in range(z.layers):
        line = jnp.zeros((z.layers, LANES), jnp.float32)
        for l in range(z.layers):
            target = l if j < half else (l + half) % z.layers
            k = (target - j) % z.layers
            weight = coupling_ref[k, target] + (1.0 if k == target else 0.0)
            line = jnp.where(layer_ids == l, weight, line)
        mix_ref[j * z.layers : (j + 1) * z.layers, :] = line
    rate = jnp.zeros((z.layers, LANES), jnp.float32)
    for l in range(z.layers):
        rate = jnp.where(layer_ids == l, 2.0 * damping_ref[l], rate)
    mix_ref[z.layers * z.layers :, :] = rate
    rate = jnp.concatenate([rate] * (z.cols // LANES), axis=1)
    for r in range(z.rows):
        tile, line = divmod(z.steps * z.rows + r, SUBLANES)
        oc = jnp.broadcast_to(own_ref[tile, line : line + 1, :], (z.layers, z.cols))
        keep = 1.0 - oc * rate
        for stage, weight in enumerate(WEIGHTS):
            oc_ref[stage * z.rows + r] = weight * oc
            keep_ref[stage * z.rows + r] = weight * keep
    for j in range(z.halo):
        for r, line in enumerate(rows_first(z, th_ref, z.section(j))):
            h_ref[j * z.rows + r] = line
    h_ref[z.halo * z.rows :] = own_ref[...]


def window_kernel(z, total_rows, first, last, target_win, *refs):
    even = lax.axis_index("lat") % 2 == 0
    h_ref, above_ref, below_ref = refs[:3]
    refs = refs[3:]
    if first:
        partner_ref, other_ref = above_ref, below_ref
        above_ref, below_ref = refs[3:5]
        refs = refs[:3] + refs[5:]
        for m in range(z.packed):
            above_ref[m] = jnp.where(even, other_ref[m], partner_ref[m])
            below_ref[m] = jnp.where(even, partner_ref[m], other_ref[m])
    own_ref = h_ref.at[pl.ds(z.halo * z.rows, (z.steps + 1) * z.tiles)]
    oc_ref, keep_ref, mix_ref = refs[:3]
    state, refs = refs[3 : 3 if first else 6], refs[3 if first else 6 :]
    if not first:
        lam_in, bias_in, refs = refs[0], refs[1], refs[2:]
        added, refs = (refs[:-8], refs[-8:]) if last else ((), refs)
        mine = lax.axis_index("win") == target_win
    if last:
        (bias_ref, lam_ref), refs = refs[:2], refs[2:]
    else:
        (bias_ref, lam_ref, main_ref, other_out), refs = refs[:4], refs[4:]
        if target_win == 1:
            partner_out, refs = refs[0], refs[1:]
    x_ref, y_ref, w_ref, sum_ref, oc_out, keep_out = refs
    halo, ext, rows, layers = z.halo, z.ext, z.rows, z.layers
    first_row = lax.axis_index("lat") * rows - halo
    parts = z.cols // LANES
    lanes = [slice(i * LANES, (i + 1) * LANES) for i in range(parts)]
    shape = (layers, LANES)
    lane_ids = lax.broadcasted_iota(jnp.int32, shape, 1)
    at_start, at_end = lane_ids == 0, lane_ids == LANES - 1
    mixers = [mix_ref[j * layers : (j + 1) * layers, :] for j in range(layers)]

    def read(ref, row):
        return [ref[row, :, lane] for lane in lanes]

    def write(ref, row, values):
        for lane, value in zip(lanes, values):
            ref[row, :, lane] = value

    def each(function, *values):
        return [function(*v) for v in zip(*values)]

    def line(k, e):
        if e < halo:
            ref, (tile, at) = above_ref, divmod(k * halo + e, SUBLANES)
            tile += z.halo_rows
        elif e >= halo + rows:
            ref, (tile, at) = below_ref, divmod(k * halo + e - halo - rows, SUBLANES)
            tile += z.halo_rows
        else:
            ref, (tile, at) = own_ref, divmod(k * rows + e - halo, SUBLANES)
        return [jnp.broadcast_to(ref[tile, at : at + 1, lane], shape) for lane in lanes]

    def add(x, y):
        return each(lambda u, v: u + v, x, y)

    def incoming(c, e):
        main_in, partner_in, other_in = state
        if not halo <= e < halo + rows:
            m = c * halo + (e if e < halo else e - halo - rows)
            pair, rest = read(partner_in, m), read(other_in, m)
            swap = even if e < halo else jnp.logical_not(even)
            return each(lambda u, v: jnp.where(swap, v, u), pair, rest)
        return read(main_in, c * rows + e - halo)

    def east(values):
        out = []
        for i, value in enumerate(values):
            after = jnp.where(at_start, values[(i + 1) % parts], value)
            before = jnp.where(at_end, values[i - 1], value)
            out.append(pltpu.roll(after, LANES - 1, axis=1) - pltpu.roll(before, 1, axis=1))
        return out

    def mixed(value):
        half = layers // 2
        low, high = mixers[0] * value, mixers[half] * value
        for k in range(1, half):
            turned = pltpu.roll(value, k, axis=0)
            low = low + mixers[k] * turned
            high = high + mixers[half + k] * turned
        return low + pltpu.roll(high, half, axis=0)

    zero = [jnp.zeros(shape, jnp.float32)] * parts
    for e in range(ext):
        a, p, q = (zero, zero, zero) if first else (incoming(c, e) for c in range(3))
        write(x_ref, e, add(a, line(0, e)))
        write(x_ref, ext + e, p)
        write(x_ref, 2 * ext + e, q)
    rate = mix_ref[layers * layers :, :]
    for i in range(2 * halo):
        oc = line(z.steps, i if i < halo else rows + i)
        keep = each(lambda v: 1.0 - v * rate, oc)
        for stage, weight in enumerate(WEIGHTS):
            write(oc_out, stage * 2 * halo + i, each(lambda v: weight * v, oc))
            write(keep_out, stage * 2 * halo + i, each(lambda v: weight * v, keep))

    def factors(stage, e):
        if halo <= e < halo + rows:
            return (read(ref, stage * rows + e - halo) for ref in (oc_ref, keep_ref))
        i = e if e < halo else e - rows
        return (read(ref, stage * 2 * halo + i) for ref in (oc_out, keep_out))

    def thickness(j, e):
        if e < halo:
            return read(above_ref, z.first[j] + e - j)
        if e >= halo + rows:
            return read(below_ref, z.first[j] + e - halo - rows)
        return read(h_ref, j * rows + e - halo)

    def run(j):
        order, stage = divmod(j, STAGES)
        source = (x_ref, y_ref, w_ref)[stage]
        target = (y_ref, w_ref, x_ref)[stage]
        low, high = j + 1, ext - j - 1

        def weighted(e, values):
            return each(lambda h, v: h * v, thickness(j, e), values)

        def body(e, carry):
            place = e - halo if halo <= e < halo + rows else None
            b_before, b_here, a_here, q_before, q_here = carry
            a_after, q_after = read(source, e + 1), read(source, 2 * ext + e + 1)
            b_after = weighted(e + 1, a_after)
            p_here = read(source, ext + e)
            oc, keep = factors(stage, e)
            row = jnp.asarray(first_row + e).astype(jnp.float32)
            coriolis = 2.0 * (0.3 + 0.4 * (row * (1.0 / total_rows) - 0.5))
            divergence = each(lambda x, n, s: x + (n - s), east(p_here), q_after, q_before)
            a = each(lambda k, v, o, m: k * v + o * mixed(m), keep, a_here, oc, divergence)
            p = each(lambda k, v, o, d, u: k * v + o * (d + coriolis * u), keep, p_here, oc, east(b_here), q_here)
            q = each(
                lambda k, v, o, n, s, u: k * v + o * ((n - s) - coriolis * u),
                keep, q_here, oc, b_after, b_before, p_here,
            )
            if stage:
                rest = 1.0 - WEIGHTS[stage]
                start = [read(x_ref, c * ext + e) for c in range(3)]
                a, p, q = (each(lambda s, v: rest * s + v, start[c], v) for c, v in enumerate((a, p, q)))
            if stage == STAGES - 1:
                if place is not None:
                    part = each(lambda v: STEP_DT * v, a)
                    if order > 0:
                        part = add(part, read(sum_ref, place))
                    if order < z.steps - 1:
                        write(sum_ref, place, part)
                    else:
                        if not first:
                            before = read(bias_in, place)
                            for ref in added:
                                before = add(before, read(ref, place))
                            part = each(lambda v, o: jnp.where(mine, v, o), part, before)
                        write(bias_ref, place, part)
                    if order == z.steps - 1:
                        for c, value in enumerate((a, p, q)):
                            if not last:
                                write(main_ref, c * rows + place, value)
                            if not first:
                                old = read(lam_in, c * rows + place)
                                value = each(lambda v, o: jnp.where(mine, v, o), value, old)
                            write(lam_ref, c * rows + place, value)
                if order < z.steps - 1:
                    a = add(a, line(order + 1, e))
            if j < halo - 1:
                for c, value in enumerate((a, p, q)):
                    write(target, c * ext + e, value)
            return b_here, b_after, a_after, q_here, q_after

        a_first = read(source, low)
        carry = (
            weighted(low - 1, read(source, low - 1)),
            weighted(low, a_first),
            a_first,
            read(source, 2 * ext + low - 1),
            read(source, 2 * ext + low),
        )
        for e in range(low, high):
            carry = body(e, carry)

    for j in range(halo):
        run(j)
    if not last:
        for c in range(3):
            for m in range(halo):
                head, foot = main_ref[c * rows + m], main_ref[c * rows + rows - halo + m]
                other_out[c * halo + m] = jnp.where(even, head, foot)
                if target_win == 1:
                    partner_out[c * halo + m] = jnp.where(even, foot, head)


def turn_kernel(z, count, lines_ref, out_ref):
    for c in range(count):
        layers_first(z, out_ref, c * z.layers * z.rows, [lines_ref[c * z.rows + r] for r in range(z.rows)])


def call(kernel, out_shapes, in_specs, scratch=(), cost=0, limit=8 << 20, space=pltpu.VMEM):
    return pl.pallas_call(
        kernel,
        out_shape=[space(s, jnp.float32) for s in out_shapes],
        in_specs=in_specs,
        out_specs=[VMEM] * len(out_shapes),
        scratch_shapes=list(scratch),
        compiler_params=pltpu.CompilerParams(vmem_limit_bytes=limit),
        cost_estimate=pl.CostEstimate(flops=cost, bytes_accessed=4 << 20, transcendentals=0),
    )


def window_scratch(z):
    counts = [3 * z.ext] * 3 + [z.rows] + [STAGES * 2 * z.halo] * 2
    return [pltpu.VMEM((count, z.layers, z.cols), jnp.float32) for count in counts]


def per_device(thickness, obs_cells, obs_values, ocean_mask, coupling, damping):
    _, steps, stages, layers, rows, cols = thickness.shape
    z = Sizes(steps, layers, rows, cols)
    n_win, n_lat = lax.axis_size("win"), lax.axis_size("lat")
    even = lax.axis_index("lat") % 2 == 0
    flat = thickness.reshape(steps * stages * layers * rows, cols)
    cube = (layers, cols)
    count = obs_cells.shape[2]

    to_partner, to_other, own = call(
        functools.partial(pack_kernel, z),
        [(z.packed,) + cube, (z.packed,) + cube, ((steps + 1) * z.tiles,) + cube],
        [HBM] * 4,
        [
            pltpu.VMEM(flat.shape, jnp.float32),
            pltpu.VMEM((steps, count), jnp.int32),
            pltpu.VMEM((steps, count), jnp.float32),
            pltpu.VMEM((rows, cols), jnp.int32),
            pltpu.SemaphoreType.DMA((4,)),
        ],
        limit=60 << 20,
    )(flat, obs_cells[0], obs_values[0], ocean_mask)
    pairs, rests = ([(i + d, i + 1 - d) for i in range(k, n_lat - 1, 2) for d in range(2)] for k in range(2))
    near = (lax.ppermute(to_partner, "lat", pairs), lax.ppermute(to_other, "lat", rests))
    h, *tables = call(
        functools.partial(own_kernel, z),
        [
            (z.fields,) + cube,
            (STAGES * rows,) + cube,
            (STAGES * rows,) + cube,
            ((layers + 1) * layers, LANES),
        ],
        [SMEM, SMEM, VMEM, VMEM],
    )(coupling, damping, flat, own)

    straight = [(i, i) for i in range(n_lat)]

    def relay(value, source_win, target_win, among=straight):
        moves = [(source_win * n_lat + i, target_win * n_lat + j) for i, j in among]
        return lax.ppermute(value, ("win", "lat"), moves)

    one, state_rows, halo_rows = ((n,) + cube for n in (rows, 3 * rows, 3 * z.halo))

    def window(target_win, fields, state, results):
        first, last = target_win == n_win - 1, target_win == 0
        outs = [one, state_rows] if last else [one, state_rows, state_rows] + [halo_rows] * (2 if target_win == 1 else 1)
        operands = fields + tuple(tables) + state + results
        return call(
            functools.partial(window_kernel, z, n_lat * rows, first, last, target_win),
            ([(z.packed,) + cube] * 2 if first else []) + outs,
            [VMEM] * len(operands),
            window_scratch(z),
            cost=40_000_000,
        )(*operands)

    above, below, bias, lam, main, *edges = window(n_win - 1, (h,) + near, (), ())
    fields = (h, above, below)
    for source_win in range(n_win - 1, 0, -1):
        arrived = relay(main, source_win, source_win - 1)
        beside = relay(edges[0], source_win, source_win - 1, rests)
        if len(edges) > 1:
            partners = relay(edges[1], source_win, source_win - 1, pairs)
        else:
            lines = arrived.reshape((3, rows) + cube)
            edge = jnp.where(even, lines[:, rows - z.halo :], lines[:, : z.halo]).reshape(halo_rows)
            partners = relay(edge, source_win - 1, source_win - 1, pairs)
        state = (arrived, partners, beside)
        if source_win > 1:
            bias, lam, main, *edges = window(source_win - 1, fields, state, (lam, bias))
    others = n_win - 1
    added = ()
    for shift in range(1, others):
        moves = [
            ((1 + w) * n_lat + i, (1 + (w + shift) % others) * n_lat + i) for w in range(others) for i in range(n_lat)
        ]
        added += (lax.ppermute(bias, ("win", "lat"), moves),)
    mine, lam = window(0, fields, state, (lam, bias) + added)
    swap = [(a * n_lat + i, (1 - a) * n_lat + i) for a in range(2) for i in range(n_lat)]
    result = mine + sum(relay(mine, 0, target_win) for target_win in range(n_win - 1, 1, -1))
    result = result + lax.ppermute(mine, ("win", "lat"), swap)
    (lam,) = call(functools.partial(turn_kernel, z, 3), [(3 * layers * rows, cols)], [VMEM], space=jax.ShapeDtypeStruct)(lam)
    (result,) = call(functools.partial(turn_kernel, z, 1), [(layers * rows, cols)], [VMEM], space=jax.ShapeDtypeStruct)(result)
    return lam.reshape(1, 3, layers, rows, cols), result.reshape(layers, rows, cols)


def solution(mesh):
    in_specs = (
        P(("groups", "win"), None, None, None, "lat", None),
        P(("groups", "win"), None, "lat"),
        P(("groups", "win"), None, "lat"),
        P(("groups", "lat"), None),
        P(),
        P(),
    )
    out_specs = (P(("groups", "win"), None, None, "lat", None), P("groups", "lat", None))
    return jax.shard_map(
        per_device, mesh=mesh, in_specs=in_specs, out_specs=out_specs, check_vma=False
    )
```

```python
import functools

import jax
import jax.numpy as jnp
from jax import lax
from jax.experimental import pallas as pl
from jax.experimental.pallas import tpu as pltpu
from jax.sharding import PartitionSpec as P

STEP_DT = 0.2
THIRD = 1.0 / 3.0
TWO_THIRDS = 2.0 / 3.0
STAGES = 3
WEIGHTS = (1.0, 0.25, TWO_THIRDS)
SUBLANES = 8
LANES = 128

VMEM = pl.BlockSpec(memory_space=pltpu.VMEM)
HBM = pl.BlockSpec(memory_space=pltpu.HBM)
SMEM = pl.BlockSpec(memory_space=pltpu.SMEM)


class Sizes:
    def __init__(self, steps, layers, rows, cols):
        self.steps, self.layers, self.rows, self.cols = steps, layers, rows, cols
        self.halo = STAGES * steps
        self.ext = rows + 2 * self.halo
        self.first = [sum(self.halo - m for m in range(j)) for j in range(self.halo)]
        self.halo_rows = sum(self.halo - m for m in range(self.halo))
        self.tiles = rows // SUBLANES
        self.tail = -(-(steps + 1) * self.halo // SUBLANES)
        self.packed = self.halo_rows + self.tail
        self.fields = self.halo * rows + (steps + 1) * self.tiles

    def section(self, j):
        step, stage = self.steps - 1 - j // STAGES, j % STAGES
        return (step * STAGES + stage) * self.layers * self.rows


def rows_first(z, ref, base):
    lines = []
    for tile in range(z.rows // SUBLANES):
        block = jnp.stack(
            [ref[base + l * z.rows + tile * SUBLANES : base + l * z.rows + (tile + 1) * SUBLANES, :] for l in range(z.layers)]
        )
        block = jnp.swapaxes(block, 0, 1)
        lines.extend(block[m] for m in range(SUBLANES))
    return lines


def layers_first(z, ref, start, lines):
    for tile in range(z.rows // SUBLANES):
        block = jnp.swapaxes(jnp.stack(lines[tile * SUBLANES : (tile + 1) * SUBLANES]), 0, 1)
        for l in range(z.layers):
            low = start + l * z.rows + tile * SUBLANES
            ref[low : low + SUBLANES, :] = block[l]


def pack_kernel(z, th_in, cells_in, values_in, mask_in, partner_ref, other_ref, own_ref, th_ref, cells_ref, values_ref, mask_ref, sem):
    copies = [
        pltpu.make_async_copy(source, target, sem.at[i])
        for i, (source, target) in enumerate(
            ((cells_in, cells_ref), (values_in, values_ref), (mask_in, mask_ref), (th_in, th_ref))
        )
    ]
    for copy in copies:
        copy.start()
    for copy in copies[:3]:
        copy.wait()
    count = cells_ref.shape[1]
    row_ids = lax.broadcasted_iota(jnp.int32, (z.rows, count), 0)
    col_ids = lax.broadcasted_iota(jnp.int32, (z.cols, count), 0)
    for order in range(z.steps):
        step = z.steps - 1 - order
        cells = cells_ref[step : step + 1, :]
        values = values_ref[step : step + 1, :]
        by_row = jnp.where(row_ids == cells // z.cols, values, 0.0)
        by_col = jnp.where(col_ids == cells % z.cols, 1.0, 0.0).astype(jnp.bfloat16)
        field = jnp.zeros((z.rows, z.cols), jnp.float32)
        for _ in range(3):
            part = by_row.astype(jnp.bfloat16)
            by_row = by_row - part.astype(jnp.float32)
            field = field + lax.dot_general(
                part, by_col, (((1,), (1,)), ((), ())), preferred_element_type=jnp.float32
            )
        own_ref[order * z.tiles : (order + 1) * z.tiles] = field.reshape(z.tiles, SUBLANES, z.cols)
    ocean = mask_ref[...].astype(jnp.float32) * (0.5 * STEP_DT)
    own_ref[z.steps * z.tiles :] = ocean.reshape(z.tiles, SUBLANES, z.cols)
    copies[3].wait()
    even = lax.axis_index("lat") % 2 == 0
    for j in range(z.halo):
        lines, need = rows_first(z, th_ref, z.section(j)), z.halo - j
        for m in range(need):
            head, foot = lines[m], lines[z.rows - need + m]
            partner_ref[z.first[j] + m] = jnp.where(even, foot, head)
            other_ref[z.first[j] + m] = jnp.where(even, head, foot)
    for q in range(z.tail * SUBLANES):
        tile, line = divmod(q, SUBLANES)
        k, m = divmod(q, z.halo)
        head = foot = jnp.zeros((1, z.cols), jnp.float32)
        if k <= z.steps:
            places = (divmod(k * z.rows + row, SUBLANES) for row in (m, z.rows - z.halo + m))
            head, foot = (own_ref[t, at : at + 1, :] for t, at in places)
        partner_ref[z.halo_rows + tile, line : line + 1, :] = jnp.where(even, foot, head)
        other_ref[z.halo_rows + tile, line : line + 1, :] = jnp.where(even, head, foot)


def own_kernel(z, coupling_ref, damping_ref, th_ref, own_ref, h_ref, oc_ref, keep_ref, mix_ref):
    layer_ids = lax.broadcasted_iota(jnp.int32, (z.layers, LANES), 0)
    half = z.layers // 2
    for j in range(z.layers):
        line = jnp.zeros((z.layers, LANES), jnp.float32)
        for l in range(z.layers):
            target = l if j < half else (l + half) % z.layers
            k = (target - j) % z.layers
            weight = coupling_ref[k, target] + (1.0 if k == target else 0.0)
            line = jnp.where(layer_ids == l, weight, line)
        mix_ref[j * z.layers : (j + 1) * z.layers, :] = line
    rate = jnp.zeros((z.layers, LANES), jnp.float32)
    for l in range(z.layers):
        rate = jnp.where(layer_ids == l, 2.0 * damping_ref[l], rate)
    mix_ref[z.layers * z.layers :, :] = rate
    rate = jnp.concatenate([rate] * (z.cols // LANES), axis=1)
    for r in range(z.rows):
        tile, line = divmod(z.steps * z.rows + r, SUBLANES)
        oc = jnp.broadcast_to(own_ref[tile, line : line + 1, :], (z.layers, z.cols))
        keep = 1.0 - oc * rate
        for stage, weight in enumerate(WEIGHTS):
            oc_ref[stage * z.rows + r] = weight * oc
            keep_ref[stage * z.rows + r] = weight * keep
    for j in range(z.halo):
        for r, line in enumerate(rows_first(z, th_ref, z.section(j))):
            h_ref[j * z.rows + r] = line
    h_ref[z.halo * z.rows :] = own_ref[...]


def window_kernel(z, total_rows, first, last, target_win, *refs):
    even = lax.axis_index("lat") % 2 == 0
    h_ref, above_ref, below_ref = refs[:3]
    refs = refs[3:]
    if first:
        partner_ref, other_ref = above_ref, below_ref
        above_ref, below_ref = refs[3:5]
        refs = refs[:3] + refs[5:]
        for m in range(z.packed):
            above_ref[m] = jnp.where(even, other_ref[m], partner_ref[m])
            below_ref[m] = jnp.where(even, partner_ref[m], other_ref[m])
    own_ref = h_ref.at[pl.ds(z.halo * z.rows, (z.steps + 1) * z.tiles)]
    oc_ref, keep_ref, mix_ref = refs[:3]
    state, refs = refs[3 : 3 if first else 6], refs[3 if first else 6 :]
    if not first:
        lam_in, bias_in, refs = refs[0], refs[1], refs[2:]
        added, refs = (refs[:-8], refs[-8:]) if last else ((), refs)
        mine = lax.axis_index("win") == target_win
    if last:
        (bias_ref, lam_ref), refs = refs[:2], refs[2:]
    else:
        (bias_ref, lam_ref, main_ref, other_out), refs = refs[:4], refs[4:]
        if not first:
            partner_out, refs = refs[0], refs[1:]
    x_ref, y_ref, w_ref, sum_ref, oc_out, keep_out = refs
    halo, ext, rows, layers = z.halo, z.ext, z.rows, z.layers
    first_row = lax.axis_index("lat") * rows - halo
    parts = z.cols // LANES
    lanes = [slice(i * LANES, (i + 1) * LANES) for i in range(parts)]
    shape = (layers, LANES)
    lane_ids = lax.broadcasted_iota(jnp.int32, shape, 1)
    at_start, at_end = lane_ids == 0, lane_ids == LANES - 1
    mixers = [mix_ref[j * layers : (j + 1) * layers, :] for j in range(layers)]

    def read(ref, row):
        return [ref[row, :, lane] for lane in lanes]

    def write(ref, row, values):
        for lane, value in zip(lanes, values):
            ref[row, :, lane] = value

    def each(function, *values):
        return [function(*v) for v in zip(*values)]

    def line(k, e):
        if e < halo:
            ref, (tile, at) = above_ref, divmod(k * halo + e, SUBLANES)
            tile += z.halo_rows
        elif e >= halo + rows:
            ref, (tile, at) = below_ref, divmod(k * halo + e - halo - rows, SUBLANES)
            tile += z.halo_rows
        else:
            ref, (tile, at) = own_ref, divmod(k * rows + e - halo, SUBLANES)
        return [jnp.broadcast_to(ref[tile, at : at + 1, lane], shape) for lane in lanes]

    def add(x, y):
        return each(lambda u, v: u + v, x, y)

    def incoming(c, e):
        main_in, partner_in, other_in = state
        if not halo <= e < halo + rows:
            m = c * halo + (e if e < halo else e - halo - rows)
            pair, rest = read(partner_in, m), read(other_in, m)
            swap = even if e < halo else jnp.logical_not(even)
            return each(lambda u, v: jnp.where(swap, v, u), pair, rest)
        return read(main_in, c * rows + e - halo)

    def east(values):
        out = []
        for i, value in enumerate(values):
            after = jnp.where(at_start, values[(i + 1) % parts], value)
            before = jnp.where(at_end, values[i - 1], value)
            out.append(pltpu.roll(after, LANES - 1, axis=1) - pltpu.roll(before, 1, axis=1))
        return out

    def mixed(value):
        half = layers // 2
        low, high = mixers[0] * value, mixers[half] * value
        for k in range(1, half):
            turned = pltpu.roll(value, k, axis=0)
            low = low + mixers[k] * turned
            high = high + mixers[half + k] * turned
        return low + pltpu.roll(high, half, axis=0)

    zero = [jnp.zeros(shape, jnp.float32)] * parts
    for e in range(ext):
        a, p, q = (zero, zero, zero) if first else (incoming(c, e) for c in range(3))
        write(x_ref, e, add(a, line(0, e)))
        write(x_ref, ext + e, p)
        write(x_ref, 2 * ext + e, q)
    rate = mix_ref[layers * layers :, :]
    for i in range(2 * halo):
        oc = line(z.steps, i if i < halo else rows + i)
        keep = each(lambda v: 1.0 - v * rate, oc)
        for stage, weight in enumerate(WEIGHTS):
            write(oc_out, stage * 2 * halo + i, each(lambda v: weight * v, oc))
            write(keep_out, stage * 2 * halo + i, each(lambda v: weight * v, keep))

    def factors(stage, e):
        if halo <= e < halo + rows:
            return (read(ref, stage * rows + e - halo) for ref in (oc_ref, keep_ref))
        i = e if e < halo else e - rows
        return (read(ref, stage * 2 * halo + i) for ref in (oc_out, keep_out))

    def thickness(j, e):
        if e < halo:
            return read(above_ref, z.first[j] + e - j)
        if e >= halo + rows:
            return read(below_ref, z.first[j] + e - halo - rows)
        return read(h_ref, j * rows + e - halo)

    def run(j):
        order, stage = divmod(j, STAGES)
        source = (x_ref, y_ref, w_ref)[stage]
        target = (y_ref, w_ref, x_ref)[stage]
        low, high = j + 1, ext - j - 1

        def weighted(e, values):
            return each(lambda h, v: h * v, thickness(j, e), values)

        def body(e, carry):
            place = e - halo if halo <= e < halo + rows else None
            b_before, b_here, a_here, q_before, q_here = carry
            a_after, q_after = read(source, e + 1), read(source, 2 * ext + e + 1)
            b_after = weighted(e + 1, a_after)
            p_here = read(source, ext + e)
            oc, keep = factors(stage, e)
            row = jnp.asarray(first_row + e).astype(jnp.float32)
            coriolis = 2.0 * (0.3 + 0.4 * (row * (1.0 / total_rows) - 0.5))
            divergence = each(lambda x, n, s: x + (n - s), east(p_here), q_after, q_before)
            a = each(lambda k, v, o, m: k * v + o * mixed(m), keep, a_here, oc, divergence)
            p = each(lambda k, v, o, d, u: k * v + o * (d + coriolis * u), keep, p_here, oc, east(b_here), q_here)
            q = each(
                lambda k, v, o, n, s, u: k * v + o * ((n - s) - coriolis * u),
                keep, q_here, oc, b_after, b_before, p_here,
            )
            if stage:
                rest = 1.0 - WEIGHTS[stage]
                start = [read(x_ref, c * ext + e) for c in range(3)]
                a, p, q = (each(lambda s, v: rest * s + v, start[c], v) for c, v in enumerate((a, p, q)))
            if stage == STAGES - 1:
                if place is not None:
                    part = each(lambda v: STEP_DT * v, a)
                    if order > 0:
                        part = add(part, read(sum_ref, place))
                    if order < z.steps - 1:
                        write(sum_ref, place, part)
                    else:
                        if not first:
                            before = read(bias_in, place)
                            for ref in added:
                                before = add(before, read(ref, place))
                            part = each(lambda v, o: jnp.where(mine, v, o), part, before)
                        write(bias_ref, place, part)
                    if order == z.steps - 1:
                        for c, value in enumerate((a, p, q)):
                            if not last:
                                write(main_ref, c * rows + place, value)
                            if not first:
                                old = read(lam_in, c * rows + place)
                                value = each(lambda v, o: jnp.where(mine, v, o), value, old)
                            write(lam_ref, c * rows + place, value)
                if order < z.steps - 1:
                    a = add(a, line(order + 1, e))
            if j < halo - 1:
                for c, value in enumerate((a, p, q)):
                    write(target, c * ext + e, value)
            return b_here, b_after, a_after, q_here, q_after

        a_first = read(source, low)
        carry = (
            weighted(low - 1, read(source, low - 1)),
            weighted(low, a_first),
            a_first,
            read(source, 2 * ext + low - 1),
            read(source, 2 * ext + low),
        )
        for e in range(low, high):
            carry = body(e, carry)

    for j in range(halo):
        run(j)
    if not last:
        for c in range(3):
            for m in range(halo):
                head, foot = main_ref[c * rows + m], main_ref[c * rows + rows - halo + m]
                other_out[c * halo + m] = jnp.where(even, head, foot)
                if not first:
                    partner_out[c * halo + m] = jnp.where(even, foot, head)


def turn_kernel(z, count, lines_ref, out_ref):
    for c in range(count):
        layers_first(z, out_ref, c * z.layers * z.rows, [lines_ref[c * z.rows + r] for r in range(z.rows)])


def call(kernel, out_shapes, in_specs, scratch=(), cost=0, limit=8 << 20, space=pltpu.VMEM):
    return pl.pallas_call(
        kernel,
        out_shape=[space(s, jnp.float32) for s in out_shapes],
        in_specs=in_specs,
        out_specs=[VMEM] * len(out_shapes),
        scratch_shapes=list(scratch),
        compiler_params=pltpu.CompilerParams(vmem_limit_bytes=limit),
        cost_estimate=pl.CostEstimate(flops=cost, bytes_accessed=4 << 20, transcendentals=0),
    )


def window_scratch(z):
    counts = [3 * z.ext] * 3 + [z.rows] + [STAGES * 2 * z.halo] * 2
    return [pltpu.VMEM((count, z.layers, z.cols), jnp.float32) for count in counts]


def per_device(thickness, obs_cells, obs_values, ocean_mask, coupling, damping):
    _, steps, stages, layers, rows, cols = thickness.shape
    z = Sizes(steps, layers, rows, cols)
    n_win, n_lat = lax.axis_size("win"), lax.axis_size("lat")
    even = lax.axis_index("lat") % 2 == 0
    flat = thickness.reshape(steps * stages * layers * rows, cols)
    cube = (layers, cols)
    count = obs_cells.shape[2]

    to_partner, to_other, own = call(
        functools.partial(pack_kernel, z),
        [(z.packed,) + cube, (z.packed,) + cube, ((steps + 1) * z.tiles,) + cube],
        [HBM] * 4,
        [
            pltpu.VMEM(flat.shape, jnp.float32),
            pltpu.VMEM((steps, count), jnp.int32),
            pltpu.VMEM((steps, count), jnp.float32),
            pltpu.VMEM((rows, cols), jnp.int32),
            pltpu.SemaphoreType.DMA((4,)),
        ],
        limit=60 << 20,
    )(flat, obs_cells[0], obs_values[0], ocean_mask)
    pairs, rests = ([(i + d, i + 1 - d) for i in range(k, n_lat - 1, 2) for d in range(2)] for k in range(2))
    near = (lax.ppermute(to_partner, "lat", pairs), lax.ppermute(to_other, "lat", rests))
    h, *tables = call(
        functools.partial(own_kernel, z),
        [
            (z.fields,) + cube,
            (STAGES * rows,) + cube,
            (STAGES * rows,) + cube,
            ((layers + 1) * layers, LANES),
        ],
        [SMEM, SMEM, VMEM, VMEM],
    )(coupling, damping, flat, own)

    straight = [(i, i) for i in range(n_lat)]

    def relay(value, source_win, target_win, among=straight):
        moves = [(source_win * n_lat + i, target_win * n_lat + j) for i, j in among]
        return lax.ppermute(value, ("win", "lat"), moves)

    one, state_rows, halo_rows = ((n,) + cube for n in (rows, 3 * rows, 3 * z.halo))

    def window(target_win, fields, state, results):
        first, last = target_win == n_win - 1, target_win == 0
        outs = [one, state_rows] if last else [one, state_rows, state_rows] + [halo_rows] * (1 if first else 2)
        operands = fields + tuple(tables) + state + results
        return call(
            functools.partial(window_kernel, z, n_lat * rows, first, last, target_win),
            ([(z.packed,) + cube] * 2 if first else []) + outs,
            [VMEM] * len(operands),
            window_scratch(z),
            cost=40_000_000,
        )(*operands)

    above, below, bias, lam, main, *edges = window(n_win - 1, (h,) + near, (), ())
    fields = (h, above, below)
    for source_win in range(n_win - 1, 0, -1):
        arrived = relay(main, source_win, source_win - 1)
        beside = relay(edges[0], source_win, source_win - 1, rests)
        if len(edges) > 1:
            partners = relay(edges[1], source_win, source_win - 1, pairs)
        else:
            lines = arrived.reshape((3, rows) + cube)
            edge = jnp.where(even, lines[:, rows - z.halo :], lines[:, : z.halo]).reshape(halo_rows)
            partners = relay(edge, source_win - 1, source_win - 1, pairs)
        state = (arrived, partners, beside)
        if source_win > 1:
            bias, lam, main, *edges = window(source_win - 1, fields, state, (lam, bias))
    others = n_win - 1
    added = ()
    for shift in range(1, others):
        moves = [
            ((1 + w) * n_lat + i, (1 + (w + shift) % others) * n_lat + i) for w in range(others) for i in range(n_lat)
        ]
        added += (lax.ppermute(bias, ("win", "lat"), moves),)
    mine, lam = window(0, fields, state, (lam, bias) + added)
    swap = [(a * n_lat + i, (1 - a) * n_lat + i) for a in range(2) for i in range(n_lat)]
    result = mine + sum(relay(mine, 0, target_win) for target_win in range(n_win - 1, 1, -1))
    result = result + lax.ppermute(mine, ("win", "lat"), swap)
    (lam,) = call(functools.partial(turn_kernel, z, 3), [(3 * layers * rows, cols)], [VMEM], space=jax.ShapeDtypeStruct)(lam)
    (result,) = call(functools.partial(turn_kernel, z, 1), [(layers * rows, cols)], [VMEM], space=jax.ShapeDtypeStruct)(result)
    return lam.reshape(1, 3, layers, rows, cols), result.reshape(layers, rows, cols)


def solution(mesh):
    in_specs = (
        P(("groups", "win"), None, None, None, "lat", None),
        P(("groups", "win"), None, "lat"),
        P(("groups", "win"), None, "lat"),
        P(("groups", "lat"), None),
        P(),
        P(),
    )
    out_specs = (P(("groups", "win"), None, None, "lat", None), P("groups", "lat", None))
    return jax.shard_map(
        per_device, mesh=mesh, in_specs=in_specs, out_specs=out_specs, check_vma=False
    )
```
